32 devices in a mesh: grp: 2 (over y), lat: 4 (over z), chan: 2 (over core), ens: 2 (over x).
Axes of the slice: x: 2, y: 2, z: 4, core: 2. Of those that a mesh axis runs over, the one named last changes fastest.
Arguments:
- grad_out: bfloat16 [4, 24, 48, 384], P(('grp', 'ens'), 'lat', None, 'chan'), parts along dimension 0, may hold values from -6 to 6
- pre_act: bfloat16 [4, 24, 48, 384], P(('grp', 'ens'), 'lat', None, 'chan'), parts along dimension 0, may hold values from -6 to 6
- coeffs: bfloat16 [4, 24, 24, 2, 384], P(('grp', 'ens'), ('lat', 'chan')), parts along dimension 0, may hold values from -6 to 6
- legendre: bfloat16 [24, 24, 24], P(('lat', 'chan'), None, 'ens'), may hold values from -1.25 to 1.25
- mixing: bfloat16 [384, 384], replicated, may hold values from -0.3125 to 0.3125
Outputs:
- grad_in: bfloat16 [4, 24, 48, 384], P(('grp', 'ens'), 'lat', None, 'chan'), parts along dimension 0
- mixing_grad: float32 [768, 384], P('grp'), parts along dimension 0
The draws below stay inside these ranges and needn't reach their ends.
There are 2 independent parts, one for each index of `grp`. The reference program is written for one: setup_inputs(seed, part) draws one part's arguments, and reference() takes and returns one part's arrays. A program takes and returns all parts, laid end to end along the dimension named above; an argument that names none is the same for every part. Nothing has to cross between parts.
All inputs are finite; a program needn't handle non-finite values.
Results may differ from the reference program's by a relative error of at most 0.0074.
Values may be sent and summed in bfloat16 or wider, within the bound.
A program may use at most 64 MiB of HBM per device.

```python
import math
import jax
import jax.numpy as jnp
from jax import lax

C = 384
NLAT = 24
NLON = 48
MODES = 24
DEGREES = 24
ENS = 2


def block_scale(key, extent, cuts, low, top_value):
    loudness, own = 1.0, jax.random.fold_in(key, 6)
    for position, shards_of in cuts:
        steps = jnp.exp(jax.random.uniform(jax.random.fold_in(own, position), (shards_of,), jnp.float32, low / len(cuts), top_value / len(cuts)))
        loudness = loudness * jnp.repeat(steps, extent[position] // shards_of).reshape([-1 if axis == position else 1 for axis in range(len(extent))])
    return loudness


def gaussian(stream_key, dims, scale, bound, pieces=(), kind=jnp.bfloat16):
    values = jax.random.normal(stream_key, dims, jnp.float32) * scale
    if len(pieces) > 0:
        values = block_scale(stream_key, dims, pieces, -0.22, 0.18) * values
    return jnp.clip(values, min=-bound, max=bound).astype(kind)


def setup_inputs(seed: int = 0, part: int = 0) -> dict:
    splits = jax.random.split(jax.random.key(seed), 6)
    part_splits = jax.random.split(jax.random.fold_in(splits[5], part), 6)
    grad_out = gaussian(part_splits[0], (ENS, NLAT, NLON, C), 1.0, 6.0, ((0, 2), (1, 4), (3, 2)))
    pre_act = gaussian(part_splits[1], (ENS, NLAT, NLON, C), 1.5, 6.0, ((0, 2), (1, 4), (3, 2)))
    coeffs = gaussian(part_splits[2], (ENS, MODES, DEGREES, 2, C), 1.0, 6.0, ((0, 2), (1, 8)))
    legendre = gaussian(splits[3], (MODES, DEGREES, NLAT), NLAT ** -0.5, 1.25, ((0, 8), (2, 2)))
    mixing = gaussian(splits[4], (C, C), C ** -0.5, 0.3125)
    return dict(grad_out=grad_out, pre_act=pre_act, coeffs=coeffs, legendre=legendre, mixing=mixing)


def fourier_table(lon_count, mode_count):
    longitude = jnp.arange(lon_count, dtype=jnp.int32)[:, None]
    wavenumber = jnp.arange(mode_count, dtype=jnp.int32)[None, :]
    product_index = longitude * wavenumber % lon_count
    angles = 2.0 * math.pi / lon_count * product_index.astype(jnp.float32)
    factor = math.sqrt(2.0 / lon_count)
    stacked = jnp.stack([jnp.cos(angles), -jnp.sin(angles)], axis=2) * factor
    return stacked.reshape(lon_count, 2 * mode_count).astype(jnp.bfloat16)

def silu_backward(cotangent, preact):
    values = preact.astype(jnp.float32)
    gate_value = jax.nn.sigmoid(values)
    return (cotangent.astype(jnp.float32) * gate_value * (1.0 + values * (1.0 - gate_value))).astype(jnp.bfloat16)

def reference(grad_out, pre_act, coeffs, legendre, mixing):
    fourier = fourier_table(NLON, MODES)
    fourier_wide = fourier.astype(jnp.float32)
    legendre_wide = legendre.astype(jnp.float32)
    weight_scale = 1.0 / (ENS * MODES)

    def member(member_data):
        cotangent, preact, stored = member_data
        scaled = silu_backward(cotangent, preact)
        spectral = jnp.einsum('nk,anc->akc', fourier_wide, scaled.astype(jnp.float32)).astype(jnp.bfloat16)
        spectral = spectral.reshape(NLAT, MODES, 2, C)
        coef_grad = jnp.einsum('mla,amrc->mlrc', legendre_wide, spectral.astype(jnp.float32)).astype(jnp.bfloat16)
        flat_grad = coef_grad.reshape(-1, C)
        weight_grad = jnp.dot(stored.reshape(-1, C).T, flat_grad, preferred_element_type=jnp.float32) * weight_scale
        mixed_grad = jnp.dot(flat_grad, mixing.T, preferred_element_type=jnp.float32).astype(jnp.bfloat16)
        mixed_grad = mixed_grad.reshape(MODES, DEGREES, 2, C)
        returned = jnp.einsum('mla,mlrc->amrc', legendre_wide, mixed_grad.astype(jnp.float32)).astype(jnp.bfloat16)
        returned = returned.reshape(NLAT, 2 * MODES, C)
        spatial = jnp.einsum('nk,akc->anc', fourier_wide, returned.astype(jnp.float32))
        result = (cotangent.astype(jnp.float32) + spatial).astype(jnp.bfloat16)
        return (result, weight_grad)
    results, weight_grads = lax.map(member, (grad_out, pre_act, coeffs))
    return (results, lax.optimization_barrier(jnp.sum(weight_grads, axis=0)))
```

```python
import math

import jax
import jax.numpy as jnp
import numpy as np
from jax import lax
from jax.experimental import pallas as pl
from jax.experimental.pallas import tpu as pltpu
from jax.sharding import PartitionSpec as P


def fourier_table(lon_count, mode_count):
    longitude = jnp.arange(lon_count, dtype=jnp.int32)[:, None]
    wavenumber = jnp.arange(mode_count, dtype=jnp.int32)[None, :]
    product_index = longitude * wavenumber % lon_count
    angles = 2.0 * math.pi / lon_count * product_index.astype(jnp.float32)
    factor = math.sqrt(2.0 / lon_count)
    stacked = jnp.stack([jnp.cos(angles), -jnp.sin(angles)], axis=2) * factor
    return stacked.reshape(lon_count, 2 * mode_count).astype(jnp.bfloat16)


def silu_backward(cotangent, preact):
    values = preact.astype(jnp.float32)
    gate_value = jax.nn.sigmoid(values)
    return (
        cotangent.astype(jnp.float32) * gate_value * (1.0 + values * (1.0 - gate_value))
    ).astype(jnp.bfloat16)


def on_device(grad_out, pre_act, coeffs, legendre, mixing):
    lat_rows = grad_out.shape[1]
    lon_count = grad_out.shape[2]
    chan_cols = grad_out.shape[3]
    mode_count = lon_count // 2
    lat_devices = lax.axis_size("lat")
    chan_count = lax.axis_size("chan")
    members = lax.axis_size("ens")
    lat_count = lat_rows * lat_devices
    channels = chan_cols * chan_count
    mode_width = 2 * mode_count // (lat_devices * chan_count)
    local_modes = mode_width // 2
    fourier = fourier_table(lon_count, mode_count)
    scaled = silu_backward(grad_out[0], pre_act[0])
    spectral = jnp.einsum(
        "nk,anc->akc", fourier, scaled, preferred_element_type=jnp.float32
    ).astype(jnp.bfloat16)
    exchanged = lax.all_to_all(
        lax.all_to_all(spectral, "lat", split_axis=1, concat_axis=0, tiled=True),
        "chan",
        split_axis=1,
        concat_axis=2,
        tiled=True,
    )
    spectral_modes = exchanged.reshape(lat_count, local_modes, 2, channels)
    legendre_full = lax.all_gather(legendre, "ens", axis=2, tiled=True)
    coef_grad = jnp.einsum(
        "mla,amrc->mlrc", legendre_full, spectral_modes, preferred_element_type=jnp.float32
    ).astype(jnp.bfloat16)
    stored = coeffs[0].reshape(-1, channels)
    flat_grad = coef_grad.reshape(-1, channels)
    weight_grad = lax.dot_general(
        stored, flat_grad, (((0,), (0,)), ((), ())), preferred_element_type=jnp.float32
    )
    weight_grad = weight_grad * (1.0 / (members * mode_count))
    weight_grad = lax.psum(weight_grad, ("lat", "chan", "ens"))
    mixed_grad = lax.dot_general(
        coef_grad, mixing, (((3,), (1,)), ((), ())), preferred_element_type=jnp.float32
    ).astype(jnp.bfloat16)
    returned = jnp.einsum(
        "mla,mlrc->amrc", legendre_full, mixed_grad, preferred_element_type=jnp.float32
    ).astype(jnp.bfloat16)
    shaped = returned.reshape(lat_count, 1, mode_width, channels)
    received = lax.all_to_all(
        lax.all_to_all(shaped, "lat", split_axis=0, concat_axis=1, tiled=True),
        "chan",
        split_axis=3,
        concat_axis=2,
        tiled=True,
    )
    row_coeffs = received.reshape(lat_rows, 2 * mode_count, chan_cols)
    spatial = jnp.einsum("nk,akc->anc", fourier, row_coeffs, preferred_element_type=jnp.float32)
    result = (grad_out[0].astype(jnp.float32) + spatial).astype(jnp.bfloat16)
    return (result[None], weight_grad)

MESH = pl.DeviceIdType.MESH
BF16 = jnp.bfloat16
F32 = jnp.float32


def dot(a, b, dims=((1,), (0,))):
    return lax.dot_general(a, b, (dims, ((), ())), preferred_element_type=F32)


def tables(rows, lon, lats, chans, members, modes, degrees):
    owners = lats * chans
    width = 2 * modes
    pad = -(-rows * width // 16) * 16
    n = np.arange(lon)[:, None]
    m = np.arange(lon // 2)[None, :]
    angles = np.float32(2.0 * math.pi / lon) * (n * m % lon).astype(np.float32)
    table = np.stack([np.cos(angles), -np.sin(angles)], axis=2).reshape(lon, lon)
    table = (table * np.float32(math.sqrt(2.0 / lon))).astype(np.float32)
    inverse = np.zeros((rows, lon, owners, pad), np.float32)
    for a in range(rows):
        for d in range(owners):
            inverse[a, :, d, a * width:(a + 1) * width] = table[:, d * width:(d + 1) * width]
    inverse = inverse.reshape(rows * lon, owners * pad)
    lat_of = np.full((lats, pad), -1)
    key_of = np.full((lats, pad), -1)
    for z in range(lats):
        for a in range(rows):
            for k in range(width):
                lat_of[z, a * width + k] = z * rows + a
                key_of[z, a * width + k] = k
    lat_of, key_of = lat_of.reshape(-1), key_of.reshape(-1)
    held = rows * lats // members
    select = (lat_of[None, :] == np.arange(members * held)[:, None]).astype(np.float32)
    select = select.reshape(members, held, -1)
    row = np.arange(modes * degrees * 2)
    spread = (row[:, None] // 2 == np.arange(modes * degrees)[None, :]).astype(np.float32)
    row_key = row // (2 * degrees) * 2 + row % 2
    mask = (row_key[:, None] == key_of[None, :]).astype(np.float32)
    cast = lambda x: jnp.asarray(np.ascontiguousarray(x), BF16)
    return (
        cast(inverse.T), cast(inverse), cast(select), cast(select.transpose(0, 2, 1)),
        cast(spread), cast(spread.T), cast(mask), cast(mask.T),
    )


def fused_kernel(
    lats, chans, members,
    grad_ref, pre_ref, coeffs_ref, leg_ref, mix_ref,
    fwd_ref, inv_ref, sel_ref, selt_ref, spread_ref, spreadt_ref, mask_ref, maskt_ref,
    out_ref, full_ref,
    lbuf, sbuf, rbuf, sbuf2, rbuf2, wown, w1s, w1r, w2own, w2s, w2r,
    lsem, esem, fsem, r1sem, r2sem, g1sem, g2sem,
):
    z, c, x = lax.axis_index("lat"), lax.axis_index("chan"), lax.axis_index("ens")
    owners, quads = lats * chans, members * chans
    me, quad = z * chans + c, x * chans + c
    pad, cols = rbuf.shape[2], rbuf.shape[3]

    def owner_peer(p):
        q = lax.rem(me + p, owners)
        return q, q // chans, lax.rem(q, chans)

    def quad_peer(p):
        q = lax.rem(quad + p, quads)
        return q, q // chans, lax.rem(q, chans)

    barrier = pltpu.get_barrier_semaphore()
    for p in range(1, owners):
        _, pz, pc = owner_peer(p)
        pl.semaphore_signal(barrier, inc=1, device_id={"lat": pz, "chan": pc}, device_id_type=MESH)
    for p in range(1, members):
        for pc in range(chans):
            target = {"ens": lax.rem(x + p, members), "chan": pc}
            pl.semaphore_signal(barrier, inc=1, device_id=target, device_id_type=MESH)

    values = pre_ref[...].astype(F32)
    gate = jax.nn.sigmoid(values)
    scaled = (grad_ref[...].astype(F32) * gate * (1.0 + values * (1.0 - gate))).astype(BF16)
    sbuf[...] = dot(fwd_ref[...], scaled).astype(BF16).reshape(owners, pad, cols)

    pl.semaphore_wait(barrier, owners - 1 + (members - 1) * chans)

    def remote(src, dst, sems, target):
        return pltpu.make_async_remote_copy(
            src_ref=src, dst_ref=dst, send_sem=sems[0], recv_sem=sems[1],
            device_id=target, device_id_type=MESH,
        )

    def pair(sem, *index):
        return sem.at[(0,) + index], sem.at[(1,) + index]

    started = []
    first = []
    for p in range(1, owners):
        q, pz, pc = owner_peer(p)
        copy = remote(sbuf.at[q], rbuf.at[c, z], pair(esem, p - 1), {"lat": pz, "chan": pc})
        copy.start()
        first.append(copy)
    legs = remote(leg_ref, lbuf, pair(lsem, 0), {"ens": lax.rem(x + 1, members)})
    legs.start()
    started += first + [legs]
    rbuf[c, z] = sbuf[me]
    legs.wait_recv()
    other = lax.rem(x + 1, members)
    mine, theirs = leg_ref[...], lbuf[...]
    by_lat = dot(mine, sel_ref[x]) + dot(theirs, sel_ref[other])
    analysis = (dot(spread_ref[...], by_lat.astype(BF16)) * mask_ref[...].astype(F32)).astype(BF16)
    across = ((1,), (1,))
    by_row = dot(selt_ref[x], mine, across) + dot(selt_ref[other], theirs, across)
    synthesis = (dot(by_row.astype(BF16), spreadt_ref[...]) * maskt_ref[...].astype(F32)).astype(BF16)

    for copy in first:
        copy.wait_recv()
    halves = [dot(analysis, rbuf[h].reshape(lats * pad, cols)) for h in range(chans)]
    coef = jnp.concatenate(halves, axis=1).astype(BF16)

    weight = dot(coeffs_ref[...], coef, ((0,), (0,))).reshape(w1s.shape)
    wown[...] = weight
    w1s[...] = weight.astype(BF16)
    reduce1 = []
    for p in range(1, quads):
        q, px, pc = quad_peer(p)
        copy = remote(w1s.at[q], w1r.at[p - 1], pair(r1sem, p - 1), {"ens": px, "chan": pc})
        copy.start()
        reduce1.append(copy)
    started += reduce1

    for h in range(chans):
        mixed = dot(coef, mix_ref[h * cols:(h + 1) * cols, :], across).astype(BF16)
        sbuf2[h] = dot(synthesis, mixed).astype(BF16).reshape(lats, pad, cols)
    second = []
    for p in range(1, owners):
        q, pz, pc = owner_peer(p)
        copy = remote(sbuf2.at[pc, pz], rbuf2.at[me], pair(fsem, p - 1), {"lat": pz, "chan": pc})
        copy.start()
        second.append(copy)
    started += second
    rbuf2[me] = sbuf2[c, z]

    total = wown[quad]
    for p, copy in enumerate(reduce1):
        copy.wait_recv()
        total = total + w1r[p].astype(F32)
    total = total.reshape(w2own.shape)
    w2own[...] = total
    w2s[...] = total.astype(BF16)
    reduce2 = []
    for p in range(1, lats):
        pz = lax.rem(z + p, lats)
        copy = remote(w2s.at[pz], w2r.at[p - 1], pair(r2sem, p - 1), {"lat": pz})
        copy.start()
        reduce2.append(copy)
    started += reduce2

    for copy in second:
        copy.wait_recv()
    spatial = dot(inv_ref[...], rbuf2[...].reshape(owners * pad, cols))
    out_ref[...] = (grad_ref[...].astype(F32) + spatial).astype(BF16)

    piece = w2own[z]
    for p, copy in enumerate(reduce2):
        copy.wait_recv()
        piece = piece + w2r[p].astype(F32)
    full_ref[quad, z] = piece.astype(BF16)
    gather1 = []
    for p in range(1, lats):
        pz = lax.rem(z + p, lats)
        copy = remote(full_ref.at[quad, z], full_ref.at[quad, z], pair(g1sem, p - 1), {"lat": pz})
        copy.start()
        gather1.append(copy)
    started += gather1
    gather2 = []
    for s in range(lats):
        if s > 0:
            gather1[s - 1].wait_recv()
        source = lax.rem(z + lats - s, lats)
        for p in range(1, quads):
            q, px, pc = quad_peer(p)
            block = full_ref.at[quad, source]
            copy = remote(block, block, pair(g2sem, p - 1, s), {"ens": px, "chan": pc})
            copy.start()
            gather2.append(copy)
    for copy in gather2:
        copy.wait_recv()
    started += gather2
    for copy in started:
        copy.wait_send()


def fused(grad_out, pre_act, coeffs, legendre, mixing):
    rows, lon, cols = grad_out.shape[1:]
    lats, chans = lax.axis_size("lat"), lax.axis_size("chan")
    members = lax.axis_size("ens")
    modes, degrees, held = legendre.shape
    owners, quads, channels = lats * chans, members * chans, cols * chans
    pad = -(-rows * 2 * modes // 16) * 16
    part, piece = channels // quads, channels // quads // lats
    constants = tables(rows, lon, lats, chans, members, modes, degrees)
    dma = pltpu.SemaphoreType.DMA
    vmem = pl.BlockSpec(memory_space=pltpu.VMEM)

    def kernel(*refs):
        fused_kernel(lats, chans, members, *refs)

    result, weight = pl.pallas_call(
        kernel,
        out_shape=(
            jax.ShapeDtypeStruct((rows * lon, cols), BF16),
            jax.ShapeDtypeStruct((quads, lats, piece, channels), BF16),
        ),
        in_specs=[vmem] * 13,
        out_specs=(vmem, vmem),
        scratch_shapes=[
            pltpu.VMEM((modes * degrees, held), BF16),
            pltpu.VMEM((owners, pad, cols), BF16),
            pltpu.VMEM((chans, lats, pad, cols), BF16),
            pltpu.VMEM((chans, lats, pad, cols), BF16),
            pltpu.VMEM((owners, pad, cols), BF16),
            pltpu.VMEM((quads, part, channels), F32),
            pltpu.VMEM((quads, part, channels), BF16),
            pltpu.VMEM((quads - 1, part, channels), BF16),
            pltpu.VMEM((lats, piece, channels), F32),
            pltpu.VMEM((lats, piece, channels), BF16),
            pltpu.VMEM((lats - 1, piece, channels), BF16),
            dma((2, 1)),
            dma((2, owners - 1)),
            dma((2, owners - 1)),
            dma((2, quads - 1)),
            dma((2, lats - 1)),
            dma((2, lats - 1)),
            dma((2, quads - 1, lats)),
        ],
        compiler_params=pltpu.CompilerParams(
            collective_id=0, has_side_effects=True, vmem_limit_bytes=32 << 20
        ),
    )(
        grad_out.reshape(rows * lon, cols),
        pre_act.reshape(rows * lon, cols),
        coeffs.reshape(modes * degrees * 2, channels),
        legendre.reshape(modes * degrees, held),
        mixing,
        *constants,
    )
    scale = 1.0 / (members * lon // 2)
    return (
        result.reshape(grad_out.shape),
        weight.astype(F32).reshape(channels, channels) * scale,
    )


def fits(mesh, rows, lon, channels):
    lats, chans, members = (mesh.shape[axis] for axis in ("lat", "chan", "ens"))
    return (
        members == 2 and lats * chans <= 8 and rows * lon <= 512
        and lon % 16 == 0 and channels % (members * chans * lats * 8) == 0
    )


def solution(mesh):
    placed = (
        P(("grp", "ens"), "lat", None, "chan"),
        P(("grp", "ens"), "lat", None, "chan"),
        P(("grp", "ens"), ("lat", "chan"), None, None, None),
        P(("lat", "chan"), None, "ens"),
        P(),
    )

    def local(grad_out, *rest):
        rows, lon, cols = grad_out.shape[1:]
        small = fits(mesh, rows, lon, cols * mesh.shape["chan"])
        return (fused if small else on_device)(grad_out, *rest)

    return jax.shard_map(
        local,
        mesh=mesh,
        in_specs=placed,
        out_specs=(P(("grp", "ens"), "lat", None, "chan"), P("grp", None)),
        check_vma=False,
    )
```

```python
import math

import jax
import jax.numpy as jnp
import numpy as np
from jax import lax
from jax.experimental import pallas as pl
from jax.experimental.pallas import tpu as pltpu
from jax.sharding import PartitionSpec as P


def fourier_table(lon_count, mode_count):
    longitude = jnp.arange(lon_count, dtype=jnp.int32)[:, None]
    wavenumber = jnp.arange(mode_count, dtype=jnp.int32)[None, :]
    product_index = longitude * wavenumber % lon_count
    angles = 2.0 * math.pi / lon_count * product_index.astype(jnp.float32)
    factor = math.sqrt(2.0 / lon_count)
    stacked = jnp.stack([jnp.cos(angles), -jnp.sin(angles)], axis=2) * factor
    return stacked.reshape(lon_count, 2 * mode_count).astype(jnp.bfloat16)


def silu_backward(cotangent, preact):
    values = preact.astype(jnp.float32)
    gate_value = jax.nn.sigmoid(values)
    return (
        cotangent.astype(jnp.float32) * gate_value * (1.0 + values * (1.0 - gate_value))
    ).astype(jnp.bfloat16)


def on_device(grad_out, pre_act, coeffs, legendre, mixing):
    lat_rows = grad_out.shape[1]
    lon_count = grad_out.shape[2]
    chan_cols = grad_out.shape[3]
    mode_count = lon_count // 2
    lat_devices = lax.axis_size("lat")
    chan_count = lax.axis_size("chan")
    members = lax.axis_size("ens")
    lat_count = lat_rows * lat_devices
    channels = chan_cols * chan_count
    mode_width = 2 * mode_count // (lat_devices * chan_count)
    local_modes = mode_width // 2
    fourier = fourier_table(lon_count, mode_count)
    scaled = silu_backward(grad_out[0], pre_act[0])
    spectral = jnp.einsum(
        "nk,anc->akc", fourier, scaled, preferred_element_type=jnp.float32
    ).astype(jnp.bfloat16)
    exchanged = lax.all_to_all(
        lax.all_to_all(spectral, "lat", split_axis=1, concat_axis=0, tiled=True),
        "chan",
        split_axis=1,
        concat_axis=2,
        tiled=True,
    )
    spectral_modes = exchanged.reshape(lat_count, local_modes, 2, channels)
    legendre_full = lax.all_gather(legendre, "ens", axis=2, tiled=True)
    coef_grad = jnp.einsum(
        "mla,amrc->mlrc", legendre_full, spectral_modes, preferred_element_type=jnp.float32
    ).astype(jnp.bfloat16)
    stored = coeffs[0].reshape(-1, channels)
    flat_grad = coef_grad.reshape(-1, channels)
    weight_grad = lax.dot_general(
        stored, flat_grad, (((0,), (0,)), ((), ())), preferred_element_type=jnp.float32
    )
    weight_grad = weight_grad * (1.0 / (members * mode_count))
    weight_grad = lax.psum(weight_grad, ("lat", "chan", "ens"))
    mixed_grad = lax.dot_general(
        coef_grad, mixing, (((3,), (1,)), ((), ())), preferred_element_type=jnp.float32
    ).astype(jnp.bfloat16)
    returned = jnp.einsum(
        "mla,mlrc->amrc", legendre_full, mixed_grad, preferred_element_type=jnp.float32
    ).astype(jnp.bfloat16)
    shaped = returned.reshape(lat_count, 1, mode_width, channels)
    received = lax.all_to_all(
        lax.all_to_all(shaped, "lat", split_axis=0, concat_axis=1, tiled=True),
        "chan",
        split_axis=3,
        concat_axis=2,
        tiled=True,
    )
    row_coeffs = received.reshape(lat_rows, 2 * mode_count, chan_cols)
    spatial = jnp.einsum("nk,akc->anc", fourier, row_coeffs, preferred_element_type=jnp.float32)
    result = (grad_out[0].astype(jnp.float32) + spatial).astype(jnp.bfloat16)
    return (result[None], weight_grad)

MESH = pl.DeviceIdType.MESH
BF16 = jnp.bfloat16
F32 = jnp.float32


def dot(a, b, dims=((1,), (0,))):
    return lax.dot_general(a, b, (dims, ((), ())), preferred_element_type=F32)


def tables(rows, lon, lats, chans, members, modes, degrees):
    owners = lats * chans
    width = 2 * modes
    pad = -(-rows * width // 16) * 16
    n = np.arange(lon)[:, None]
    m = np.arange(lon // 2)[None, :]
    angles = np.float32(2.0 * math.pi / lon) * (n * m % lon).astype(np.float32)
    table = np.stack([np.cos(angles), -np.sin(angles)], axis=2).reshape(lon, lon)
    table = (table * np.float32(math.sqrt(2.0 / lon))).astype(np.float32)
    inverse = np.zeros((rows, lon, owners, pad), np.float32)
    for a in range(rows):
        for d in range(owners):
            inverse[a, :, d, a * width:(a + 1) * width] = table[:, d * width:(d + 1) * width]
    inverse = inverse.reshape(rows * lon, owners * pad)
    lat_of = np.full((lats, pad), -1)
    key_of = np.full((lats, pad), -1)
    for z in range(lats):
        for a in range(rows):
            for k in range(width):
                lat_of[z, a * width + k] = z * rows + a
                key_of[z, a * width + k] = k
    lat_of, key_of = lat_of.reshape(-1), key_of.reshape(-1)
    held = rows * lats // members
    select = (lat_of[None, :] == np.arange(members * held)[:, None]).astype(np.float32)
    select = select.reshape(members, held, -1)
    row = np.arange(modes * degrees * 2)
    spread = (row[:, None] // 2 == np.arange(modes * degrees)[None, :]).astype(np.float32)
    row_key = row // (2 * degrees) * 2 + row % 2
    mask = (row_key[:, None] == key_of[None, :]).astype(np.float32)
    cast = lambda x: jnp.asarray(np.ascontiguousarray(x), BF16)
    return (
        cast(inverse.T), cast(inverse), cast(select), cast(select.transpose(0, 2, 1)),
        cast(spread), cast(spread.T), cast(mask), cast(mask.T),
    )


def fused_kernel(
    lats, chans, members,
    grad_hbm, pre_hbm, coeffs_hbm, leg_hbm, mix_hbm,
    fwd_hbm, inv_hbm, sel_hbm, selt_hbm, spread_hbm, spreadt_hbm, mask_hbm, maskt_hbm,
    out_hbm, full_hbm,
    out_ref, full_ref,
    grad_ref, pre_ref, coeffs_ref, leg_ref, mix_ref,
    fwd_ref, inv_ref, sel_ref, selt_ref, spread_ref, spreadt_ref, mask_ref, maskt_ref,
    stored, lbuf, sbuf, rbuf, sbuf2, rbuf2, wown, w1s, w1r, w2own, w2s, w2r,
    isem, osem, lsem, esem, fsem, r1sem, r2sem, g1sem, g2sem,
):
    z, c, x = lax.axis_index("lat"), lax.axis_index("chan"), lax.axis_index("ens")
    owners, quads = lats * chans, members * chans
    me, quad = z * chans + c, x * chans + c
    pad, cols = rbuf.shape[2], rbuf.shape[3]

    def owner_peer(p):
        q = lax.rem(me + p, owners)
        return q, q // chans, lax.rem(q, chans)

    def quad_peer(p):
        q = lax.rem(quad + p, quads)
        return q, q // chans, lax.rem(q, chans)

    sources = (
        pre_hbm, grad_hbm, fwd_hbm, leg_hbm, sel_hbm, selt_hbm, spread_hbm, spreadt_hbm,
        mask_hbm, maskt_hbm, coeffs_hbm, mix_hbm, inv_hbm,
    )
    targets = (
        pre_ref, grad_ref, fwd_ref, leg_ref, sel_ref, selt_ref, spread_ref, spreadt_ref,
        mask_ref, maskt_ref, coeffs_ref, mix_ref, inv_ref,
    )
    loads = [
        pltpu.make_async_copy(source, target, isem.at[i])
        for i, (source, target) in enumerate(zip(sources, targets))
    ]
    for load in loads:
        load.start()
    barrier = pltpu.get_barrier_semaphore()
    for p in range(1, owners):
        _, pz, pc = owner_peer(p)
        pl.semaphore_signal(barrier, inc=1, device_id={"lat": pz, "chan": pc}, device_id_type=MESH)
    for p in range(1, members):
        for pc in range(chans):
            target = {"ens": lax.rem(x + p, members), "chan": pc}
            pl.semaphore_signal(barrier, inc=1, device_id=target, device_id_type=MESH)

    for load in loads[:3]:
        load.wait()
    values = pre_ref[...].astype(F32)
    gate = jax.nn.sigmoid(values)
    scaled = (grad_ref[...].astype(F32) * gate * (1.0 + values * (1.0 - gate))).astype(BF16)
    sbuf[...] = dot(fwd_ref[...], scaled).astype(BF16).reshape(owners, pad, cols)

    pl.semaphore_wait(barrier, owners - 1 + (members - 1) * chans)

    def remote(src, dst, sems, target):
        return pltpu.make_async_remote_copy(
            src_ref=src, dst_ref=dst, send_sem=sems[0], recv_sem=sems[1],
            device_id=target, device_id_type=MESH,
        )

    def pair(sem, *index):
        return sem.at[(0,) + index], sem.at[(1,) + index]

    started = []
    first = []
    for p in range(1, owners):
        q, pz, pc = owner_peer(p)
        copy = remote(sbuf.at[q], rbuf.at[c, z], pair(esem, p - 1), {"lat": pz, "chan": pc})
        copy.start()
        first.append(copy)
    for load in loads[3:]:
        load.wait()
    legs = remote(leg_ref, lbuf, pair(lsem, 0), {"ens": lax.rem(x + 1, members)})
    legs.start()
    started += first + [legs]
    rbuf[c, z] = sbuf[me]
    legs.wait_recv()
    other = lax.rem(x + 1, members)
    modes, degrees = leg_ref.shape[0], leg_ref.shape[2]
    by_lat, synthesis = [], 0.0
    for m in range(modes):
        mine, theirs = leg_ref[m], lbuf[m]
        down = ((0,), (0,))
        by_lat.append(dot(mine, sel_ref[x], down) + dot(theirs, sel_ref[other], down))
        by_row = dot(selt_ref[x], mine) + dot(selt_ref[other], theirs)
        rows = spreadt_ref[m * degrees:(m + 1) * degrees, :]
        synthesis = synthesis + dot(by_row.astype(BF16), rows)
    by_lat = jnp.concatenate(by_lat, axis=0).astype(BF16)
    analysis = (dot(spread_ref[...], by_lat) * mask_ref[...].astype(F32)).astype(BF16)
    synthesis = (synthesis * maskt_ref[...].astype(F32)).astype(BF16)
    across = ((1,), (1,))
    stored[...] = coeffs_ref[...].reshape(stored.shape)

    for copy in first:
        copy.wait_recv()
    halves = [dot(analysis, rbuf[h].reshape(lats * pad, cols)) for h in range(chans)]
    coef = jnp.concatenate(halves, axis=1).astype(BF16)

    weight = dot(stored[...], coef, ((0,), (0,))).reshape(w1s.shape)
    wown[...] = weight
    w1s[...] = weight.astype(BF16)
    reduce1 = []
    for p in range(1, quads):
        q, px, pc = quad_peer(p)
        copy = remote(w1s.at[q], w1r.at[p - 1], pair(r1sem, p - 1), {"ens": px, "chan": pc})
        copy.start()
        reduce1.append(copy)
    started += reduce1

    for h in range(chans):
        mixed = dot(coef, mix_ref[h * cols:(h + 1) * cols, :], across).astype(BF16)
        sbuf2[h] = dot(synthesis, mixed).astype(BF16).reshape(lats, pad, cols)
    second = []
    for p in range(1, owners):
        q, pz, pc = owner_peer(p)
        copy = remote(sbuf2.at[pc, pz], rbuf2.at[me], pair(fsem, p - 1), {"lat": pz, "chan": pc})
        copy.start()
        second.append(copy)
    started += second
    rbuf2[me] = sbuf2[c, z]

    total = wown[quad]
    for p, copy in enumerate(reduce1):
        copy.wait_recv()
        total = total + w1r[p].astype(F32)
    total = total.reshape(w2own.shape)
    w2own[...] = total
    w2s[...] = total.astype(BF16)
    reduce2 = []
    for p in range(1, lats):
        pz = lax.rem(z + p, lats)
        copy = remote(w2s.at[pz], w2r.at[p - 1], pair(r2sem, p - 1), {"lat": pz})
        copy.start()
        reduce2.append(copy)
    started += reduce2

    for copy in second:
        copy.wait_recv()
    spatial = dot(inv_ref[...], rbuf2[...].reshape(owners * pad, cols))
    out_ref[...] = (grad_ref[...].astype(F32) + spatial).astype(BF16)
    stores = [pltpu.make_async_copy(out_ref, out_hbm, osem.at[0])]
    stores[0].start()

    piece = w2own[z]
    for p, copy in enumerate(reduce2):
        copy.wait_recv()
        piece = piece + w2r[p].astype(F32)
    full_ref[quad, z] = piece.astype(BF16)
    gather1 = []
    for p in range(1, lats):
        pz = lax.rem(z + p, lats)
        copy = remote(full_ref.at[quad, z], full_ref.at[quad, z], pair(g1sem, p - 1), {"lat": pz})
        copy.start()
        gather1.append(copy)
    started += gather1
    gather2 = []
    for s in range(lats):
        if s > 0:
            gather1[s - 1].wait_recv()
        source = lax.rem(z + lats - s, lats)
        for p in range(1, quads):
            q, px, pc = quad_peer(p)
            block = full_ref.at[quad, source]
            copy = remote(block, block, pair(g2sem, p - 1, s), {"ens": px, "chan": pc})
            copy.start()
            gather2.append(copy)
    for copy in gather2:
        copy.wait_recv()
    stores.append(pltpu.make_async_copy(full_ref, full_hbm, osem.at[1]))
    stores[1].start()
    started += gather2
    for copy in started:
        copy.wait_send()
    for store in stores:
        store.wait()


def fused(grad_out, pre_act, coeffs, legendre, mixing):
    rows, lon, cols = grad_out.shape[1:]
    lats, chans = lax.axis_size("lat"), lax.axis_size("chan")
    members = lax.axis_size("ens")
    modes, degrees, held = legendre.shape
    owners, quads, channels = lats * chans, members * chans, cols * chans
    pad = -(-rows * 2 * modes // 16) * 16
    part, piece = channels // quads, channels // quads // lats
    constants = tables(rows, lon, lats, chans, members, modes, degrees)
    dma = pltpu.SemaphoreType.DMA

    def kernel(*refs):
        fused_kernel(lats, chans, members, *refs)

    operands = (
        grad_out.reshape(rows * lon, cols),
        pre_act.reshape(rows * lon, cols),
        coeffs.reshape(modes * degrees, 2, channels),
        legendre.transpose(0, 2, 1),
        mixing,
        *constants,
    )
    result, weight = pl.pallas_call(
        kernel,
        out_shape=(
            jax.ShapeDtypeStruct((rows * lon, cols), BF16),
            jax.ShapeDtypeStruct((quads, lats, piece, channels), BF16),
        ),
        in_specs=[pl.BlockSpec(memory_space=pltpu.HBM)] * 13,
        out_specs=(pl.BlockSpec(memory_space=pltpu.HBM),) * 2,
        scratch_shapes=[
            pltpu.VMEM((rows * lon, cols), BF16),
            pltpu.VMEM((quads, lats, piece, channels), BF16),
            *[pltpu.VMEM(operand.shape, BF16) for operand in operands],
            pltpu.VMEM((modes * degrees * 2, channels), BF16),
            pltpu.VMEM((modes, held, degrees), BF16),
            pltpu.VMEM((owners, pad, cols), BF16),
            pltpu.VMEM((chans, lats, pad, cols), BF16),
            pltpu.VMEM((chans, lats, pad, cols), BF16),
            pltpu.VMEM((owners, pad, cols), BF16),
            pltpu.VMEM((quads, part, channels), F32),
            pltpu.VMEM((quads, part, channels), BF16),
            pltpu.VMEM((quads - 1, part, channels), BF16),
            pltpu.VMEM((lats, piece, channels), F32),
            pltpu.VMEM((lats, piece, channels), BF16),
            pltpu.VMEM((lats - 1, piece, channels), BF16),
            dma((len(operands),)),
            dma((2,)),
            dma((2, 1)),
            dma((2, owners - 1)),
            dma((2, owners - 1)),
            dma((2, quads - 1)),
            dma((2, lats - 1)),
            dma((2, lats - 1)),
            dma((2, quads - 1, lats)),
        ],
        compiler_params=pltpu.CompilerParams(
            collective_id=0, has_side_effects=True, vmem_limit_bytes=60 << 20
        ),
    )(*operands)
    scale = 1.0 / (members * lon // 2)
    return (
        result.reshape(grad_out.shape),
        weight.astype(F32).reshape(channels, channels) * scale,
    )


def fits(mesh, rows, lon, channels):
    lats, chans, members = (mesh.shape[axis] for axis in ("lat", "chan", "ens"))
    return (
        members == 2 and lats * chans <= 8 and rows * lon <= 512
        and lon % 16 == 0 and channels % (members * chans * lats * 8) == 0
    )


def solution(mesh):
    placed = (
        P(("grp", "ens"), "lat", None, "chan"),
        P(("grp", "ens"), "lat", None, "chan"),
        P(("grp", "ens"), ("lat", "chan"), None, None, None),
        P(("lat", "chan"), None, "ens"),
        P(),
    )

    def local(grad_out, *rest):
        rows, lon, cols = grad_out.shape[1:]
        small = fits(mesh, rows, lon, cols * mesh.shape["chan"])
        return (fused if small else on_device)(grad_out, *rest)

    return jax.shard_map(
        local,
        mesh=mesh,
        in_specs=placed,
        out_specs=(P(("grp", "ens"), "lat", None, "chan"), P("grp", None)),
        check_vma=False,
    )
```

```python
import math

import jax
import jax.numpy as jnp
import numpy as np
from jax import lax
from jax.experimental import pallas as pl
from jax.experimental.pallas import tpu as pltpu
from jax.sharding import PartitionSpec as P


def fourier_table(lon_count, mode_count):
    longitude = jnp.arange(lon_count, dtype=jnp.int32)[:, None]
    wavenumber = jnp.arange(mode_count, dtype=jnp.int32)[None, :]
    product_index = longitude * wavenumber % lon_count
    angles = 2.0 * math.pi / lon_count * product_index.astype(jnp.float32)
    factor = math.sqrt(2.0 / lon_count)
    stacked = jnp.stack([jnp.cos(angles), -jnp.sin(angles)], axis=2) * factor
    return stacked.reshape(lon_count, 2 * mode_count).astype(jnp.bfloat16)


def silu_backward(cotangent, preact):
    values = preact.astype(jnp.float32)
    gate_value = jax.nn.sigmoid(values)
    return (
        cotangent.astype(jnp.float32) * gate_value * (1.0 + values * (1.0 - gate_value))
    ).astype(jnp.bfloat16)


def on_device(grad_out, pre_act, coeffs, legendre, mixing):
    lat_rows = grad_out.shape[1]
    lon_count = grad_out.shape[2]
    chan_cols = grad_out.shape[3]
    mode_count = lon_count // 2
    lat_devices = lax.axis_size("lat")
    chan_count = lax.axis_size("chan")
    members = lax.axis_size("ens")
    lat_count = lat_rows * lat_devices
    channels = chan_cols * chan_count
    mode_width = 2 * mode_count // (lat_devices * chan_count)
    local_modes = mode_width // 2
    fourier = fourier_table(lon_count, mode_count)
    scaled = silu_backward(grad_out[0], pre_act[0])
    spectral = jnp.einsum(
        "nk,anc->akc", fourier, scaled, preferred_element_type=jnp.float32
    ).astype(jnp.bfloat16)
    exchanged = lax.all_to_all(
        lax.all_to_all(spectral, "lat", split_axis=1, concat_axis=0, tiled=True),
        "chan",
        split_axis=1,
        concat_axis=2,
        tiled=True,
    )
    spectral_modes = exchanged.reshape(lat_count, local_modes, 2, channels)
    legendre_full = lax.all_gather(legendre, "ens", axis=2, tiled=True)
    coef_grad = jnp.einsum(
        "mla,amrc->mlrc", legendre_full, spectral_modes, preferred_element_type=jnp.float32
    ).astype(jnp.bfloat16)
    stored = coeffs[0].reshape(-1, channels)
    flat_grad = coef_grad.reshape(-1, channels)
    weight_grad = lax.dot_general(
        stored, flat_grad, (((0,), (0,)), ((), ())), preferred_element_type=jnp.float32
    )
    weight_grad = weight_grad * (1.0 / (members * mode_count))
    weight_grad = lax.psum(weight_grad, ("lat", "chan", "ens"))
    mixed_grad = lax.dot_general(
        coef_grad, mixing, (((3,), (1,)), ((), ())), preferred_element_type=jnp.float32
    ).astype(jnp.bfloat16)
    returned = jnp.einsum(
        "mla,mlrc->amrc", legendre_full, mixed_grad, preferred_element_type=jnp.float32
    ).astype(jnp.bfloat16)
    shaped = returned.reshape(lat_count, 1, mode_width, channels)
    received = lax.all_to_all(
        lax.all_to_all(shaped, "lat", split_axis=0, concat_axis=1, tiled=True),
        "chan",
        split_axis=3,
        concat_axis=2,
        tiled=True,
    )
    row_coeffs = received.reshape(lat_rows, 2 * mode_count, chan_cols)
    spatial = jnp.einsum("nk,akc->anc", fourier, row_coeffs, preferred_element_type=jnp.float32)
    result = (grad_out[0].astype(jnp.float32) + spatial).astype(jnp.bfloat16)
    return (result[None], weight_grad)

MESH = pl.DeviceIdType.MESH
BF16 = jnp.bfloat16
F32 = jnp.float32


def dot(a, b, dims=((1,), (0,))):
    return lax.dot_general(a, b, (dims, ((), ())), preferred_element_type=F32)


LANES = 128


def slots(rows, width):
    whole = [(a, a, k) for a in range(rows) for k in range(width)]
    paired = [(a, a + 1, k) for a in range(0, rows, 2) for k in range(width)]
    return whole, paired


def padded(rows, width):
    return -(-(rows + rows // 2) * width // 16) * 16


def tables(rows, lon, lats, chans, members, modes, degrees):
    owners = lats * chans
    width = 2 * modes
    pad = padded(rows, width)
    n = np.arange(lon)[:, None]
    m = np.arange(lon // 2)[None, :]
    angles = np.float32(2.0 * math.pi / lon) * (n * m % lon).astype(np.float32)
    table = np.stack([np.cos(angles), -np.sin(angles)], axis=2).reshape(lon, lon)
    table = (table * np.float32(math.sqrt(2.0 / lon))).astype(np.float32)
    groups = rows + rows // 2
    inverse = np.zeros((groups, lon, owners, pad), np.float32)
    for g in range(groups):
        for d in range(owners):
            inverse[g, :, d, g * width:(g + 1) * width] = table[:, d * width:(d + 1) * width]
    inverse = inverse.reshape(groups * lon, owners * pad)
    whole, paired = slots(rows, width)
    lat_of = np.full((3, lats, pad), -1)
    key_of = np.full((3, lats, pad), -1)
    for z in range(lats):
        for i, (even, odd, k) in enumerate(whole + paired):
            if i < len(whole):
                lat_of[0, z, i], key_of[0, z, i] = z * rows + even, k
            else:
                lat_of[1, z, i], key_of[1, z, i] = z * rows + even, k
                lat_of[2, z, i], key_of[2, z, i] = z * rows + odd, k
    lat_of, key_of = lat_of.reshape(-1), key_of.reshape(-1)
    held = rows * lats // members
    select = (lat_of[None, :] == np.arange(members * held)[:, None]).astype(np.float32)
    select = select.reshape(members, held, -1)
    row = np.arange(modes * degrees * 2)
    spread = (row[:, None] // 2 == np.arange(modes * degrees)[None, :]).astype(np.float32)
    row_key = row // (2 * degrees) * 2 + row % 2
    mask = (row_key[:, None] == key_of[None, :]).astype(np.float32)
    cast = lambda x: jnp.asarray(np.ascontiguousarray(x), BF16)
    return (
        cast(inverse.T), cast(inverse), cast(select), cast(select.transpose(0, 2, 1)),
        cast(spread), cast(spread.T), cast(mask), cast(mask.T),
    )


def fused_kernel(
    lats, chans, members, lon,
    grad_hbm, pre_hbm, coeffs_hbm, leg_hbm, mix_hbm,
    fwd_hbm, inv_hbm, sel_hbm, selt_hbm, spread_hbm, spreadt_hbm, mask_hbm, maskt_hbm,
    out_hbm, full_hbm,
    out_ref, full_ref, wide_ref,
    grad_ref, pre_ref, coeffs_ref, leg_ref, mix_ref,
    fwd_ref, inv_ref, sel_ref, selt_ref, spread_ref, spreadt_ref, mask_ref, maskt_ref,
    stored, lbuf, sbuf, rbuf, sbuf2, rbuf2, wown, w1s, w1r, w2own, w2s, w2r,
    isem, osem, lsem, esem, fsem, r1sem, r2sem, g1sem, g2sem,
):
    z, c, x = lax.axis_index("lat"), lax.axis_index("chan"), lax.axis_index("ens")
    owners, quads = lats * chans, members * chans
    me, quad = z * chans + c, x * chans + c
    pad, cols, blocks = rbuf.shape[2], grad_ref.shape[1], lats * rbuf.shape[2]

    def owner_peer(p):
        q = lax.rem(me + p, owners)
        return q, q // chans, lax.rem(q, chans)

    def quad_peer(p):
        q = lax.rem(quad + p, quads)
        return q, q // chans, lax.rem(q, chans)

    sources = (
        pre_hbm, grad_hbm, fwd_hbm, leg_hbm, sel_hbm, selt_hbm, spread_hbm, spreadt_hbm,
        mask_hbm, maskt_hbm, coeffs_hbm, mix_hbm, inv_hbm,
    )
    targets = (
        pre_ref, grad_ref, fwd_ref, leg_ref, sel_ref, selt_ref, spread_ref, spreadt_ref,
        mask_ref, maskt_ref, coeffs_ref, mix_ref, inv_ref,
    )
    loads = [
        pltpu.make_async_copy(source, target, isem.at[i])
        for i, (source, target) in enumerate(zip(sources, targets))
    ]
    for load in loads:
        load.start()
    barrier = pltpu.get_barrier_semaphore()
    for p in range(1, owners):
        _, pz, pc = owner_peer(p)
        pl.semaphore_signal(barrier, inc=1, device_id={"lat": pz, "chan": pc}, device_id_type=MESH)
    for p in range(1, members):
        for pc in range(chans):
            target = {"ens": lax.rem(x + p, members), "chan": pc}
            pl.semaphore_signal(barrier, inc=1, device_id=target, device_id_type=MESH)

    for load in loads[:3]:
        load.wait()
    values = pre_ref[...].astype(F32)
    gate = jax.nn.sigmoid(values)
    scaled = grad_ref[...].astype(F32) * gate * (1.0 + values * (1.0 - gate))
    points, half = scaled.shape[0], LANES // 2
    tail = scaled[:, LANES:].reshape(-1, 2, lon, half)
    paired = jnp.concatenate([tail[:, 0], tail[:, 1]], axis=-1).reshape(-1, LANES)
    packed = jnp.concatenate([scaled[:, :LANES], paired], axis=0).astype(BF16)
    sbuf[...] = dot(fwd_ref[...], packed).astype(BF16).reshape(owners, pad, LANES)

    pl.semaphore_wait(barrier, owners - 1 + (members - 1) * chans)

    def remote(src, dst, sems, target):
        return pltpu.make_async_remote_copy(
            src_ref=src, dst_ref=dst, send_sem=sems[0], recv_sem=sems[1],
            device_id=target, device_id_type=MESH,
        )

    def pair(sem, *index):
        return sem.at[(0,) + index], sem.at[(1,) + index]

    started = []
    first = []
    for p in range(1, owners):
        q, pz, pc = owner_peer(p)
        copy = remote(sbuf.at[q], rbuf.at[c, z], pair(esem, p - 1), {"lat": pz, "chan": pc})
        copy.start()
        first.append(copy)
    for load in loads[3:]:
        load.wait()
    legs = remote(leg_ref, lbuf, pair(lsem, 0), {"ens": lax.rem(x + 1, members)})
    legs.start()
    started += first + [legs]
    rbuf[c, z] = sbuf[me]
    legs.wait_recv()
    other = lax.rem(x + 1, members)
    modes, degrees = leg_ref.shape[0], leg_ref.shape[2]
    by_lat, synthesis = [], 0.0
    for m in range(modes):
        mine, theirs = leg_ref[m], lbuf[m]
        down = ((0,), (0,))
        by_lat.append(dot(mine, sel_ref[x], down) + dot(theirs, sel_ref[other], down))
        by_row = dot(selt_ref[x], mine) + dot(selt_ref[other], theirs)
        rows = spreadt_ref[m * degrees:(m + 1) * degrees, :]
        synthesis = synthesis + dot(by_row.astype(BF16), rows)
    by_lat = jnp.concatenate(by_lat, axis=0).astype(BF16)
    analysis = (dot(spread_ref[...], by_lat) * mask_ref[...].astype(F32)).astype(BF16)
    synthesis = (synthesis * maskt_ref[...].astype(F32)).astype(BF16)
    across = ((1,), (1,))
    stored[...] = coeffs_ref[...].reshape(stored.shape)

    for copy in first:
        copy.wait_recv()
    halves = []
    for h in range(chans):
        held = rbuf[h].reshape(blocks, LANES)
        wide, even, odd = (dot(analysis[:, v * blocks:(v + 1) * blocks], held) for v in range(3))
        halves += [wide, even[:, :half] + odd[:, half:]]
    coef = jnp.concatenate(halves, axis=1).astype(BF16)

    weight = dot(stored[...], coef, ((0,), (0,))).reshape(w1s.shape)
    wown[...] = weight
    w1s[...] = weight.astype(BF16)
    reduce1 = []
    for p in range(1, quads):
        q, px, pc = quad_peer(p)
        copy = remote(w1s.at[q], w1r.at[p - 1], pair(r1sem, p - 1), {"ens": px, "chan": pc})
        copy.start()
        reduce1.append(copy)
    started += reduce1

    for h in range(chans):
        mixed = dot(coef, mix_ref[h * cols:(h + 1) * cols, :], across)
        rest = mixed[:, LANES:]
        none = jnp.zeros_like(rest)
        sides = (
            mixed[:, :LANES],
            jnp.concatenate([rest, none], axis=1),
            jnp.concatenate([none, rest], axis=1),
        )
        returned = sum(
            dot(synthesis[v * blocks:(v + 1) * blocks], side.astype(BF16))
            for v, side in enumerate(sides)
        )
        sbuf2[h] = returned.astype(BF16).reshape(lats, pad, LANES)
    second = []
    for p in range(1, owners):
        q, pz, pc = owner_peer(p)
        copy = remote(sbuf2.at[pc, pz], rbuf2.at[me], pair(fsem, p - 1), {"lat": pz, "chan": pc})
        copy.start()
        second.append(copy)
    started += second
    rbuf2[me] = sbuf2[c, z]

    total = wown[quad]
    for p, copy in enumerate(reduce1):
        copy.wait_recv()
        total = total + w1r[p].astype(F32)
    total = total.reshape(w2own.shape)
    w2own[...] = total
    w2s[...] = total.astype(BF16)
    reduce2 = []
    for p in range(1, lats):
        pz = lax.rem(z + p, lats)
        copy = remote(w2s.at[pz], w2r.at[p - 1], pair(r2sem, p - 1), {"lat": pz})
        copy.start()
        reduce2.append(copy)
    started += reduce2

    for copy in second:
        copy.wait_recv()
    spatial = dot(inv_ref[...], rbuf2[...].reshape(owners * pad, LANES))
    pairs = spatial[points:].reshape(-1, 1, lon, LANES)
    rest = jnp.concatenate([pairs[..., :half], pairs[..., half:]], axis=1).reshape(points, half)
    spatial = jnp.concatenate([spatial[:points], rest], axis=1)
    out_ref[...] = (grad_ref[...].astype(F32) + spatial).astype(BF16)
    stores = [pltpu.make_async_copy(out_ref, out_hbm, osem.at[0])]
    stores[0].start()

    piece = w2own[z]
    for p, copy in enumerate(reduce2):
        copy.wait_recv()
        piece = piece + w2r[p].astype(F32)
    full_ref[quad, z] = piece.astype(BF16)
    gather1 = []
    for p in range(1, lats):
        pz = lax.rem(z + p, lats)
        copy = remote(full_ref.at[quad, z], full_ref.at[quad, z], pair(g1sem, p - 1), {"lat": pz})
        copy.start()
        gather1.append(copy)
    started += gather1
    gather2 = []
    for s in range(lats):
        if s > 0:
            gather1[s - 1].wait_recv()
        source = lax.rem(z + lats - s, lats)
        for p in range(1, quads):
            q, px, pc = quad_peer(p)
            block = full_ref.at[quad, source]
            copy = remote(block, block, pair(g2sem, p - 1, s), {"ens": px, "chan": pc})
            copy.start()
            gather2.append(copy)
    part = full_ref.shape[1] * full_ref.shape[2]
    scale = 1.0 / (members * lon // 2)
    for p in range(quads):
        if p > 0:
            for s in range(lats):
                gather2[s * (quads - 1) + p - 1].wait_recv()
        block = lax.rem(quad + quads - p, quads)
        place = pl.ds(pl.multiple_of(block * part, part), part)
        wide_ref[place, :] = full_ref[block].astype(F32).reshape(part, -1) * scale
        store = pltpu.make_async_copy(wide_ref.at[place], full_hbm.at[place], osem.at[1 + p])
        store.start()
        stores.append(store)
    started += gather2
    for copy in started:
        copy.wait_send()
    for store in stores:
        store.wait()


def copy_kernel(first_in, second_in, first_out, second_out, sem):
    copies = (
        pltpu.make_async_copy(second_in, second_out, sem.at[1]),
        pltpu.make_async_copy(first_in, first_out, sem.at[0]),
    )
    for copy in copies:
        copy.start()
    for copy in copies:
        copy.wait()


def fused(grad_out, pre_act, coeffs, legendre, mixing):
    rows, lon, cols = grad_out.shape[1:]
    lats, chans = lax.axis_size("lat"), lax.axis_size("chan")
    members = lax.axis_size("ens")
    modes, degrees, held = legendre.shape
    owners, quads, channels = lats * chans, members * chans, cols * chans
    pad = padded(rows, 2 * modes)
    part, piece = channels // quads, channels // quads // lats
    constants = tables(rows, lon, lats, chans, members, modes, degrees)
    dma = pltpu.SemaphoreType.DMA

    def kernel(*refs):
        fused_kernel(lats, chans, members, lon, *refs)

    operands = (
        grad_out.reshape(rows * lon, cols),
        pre_act.reshape(rows * lon, cols),
        coeffs.reshape(modes * degrees, 2, channels),
        legendre.transpose(0, 2, 1),
        mixing,
        *constants,
    )
    result, weight = pl.pallas_call(
        kernel,
        out_shape=(
            jax.ShapeDtypeStruct((rows * lon, cols), BF16),
            jax.ShapeDtypeStruct((channels, channels), F32),
        ),
        in_specs=[pl.BlockSpec(memory_space=pltpu.HBM)] * 13,
        out_specs=(pl.BlockSpec(memory_space=pltpu.HBM),) * 2,
        scratch_shapes=[
            pltpu.VMEM((rows * lon, cols), BF16),
            pltpu.VMEM((quads, lats, piece, channels), BF16),
            pltpu.VMEM((channels, channels), F32),
            *[pltpu.VMEM(operand.shape, BF16) for operand in operands],
            pltpu.VMEM((modes * degrees * 2, channels), BF16),
            pltpu.VMEM((modes, held, degrees), BF16),
            pltpu.VMEM((owners, pad, LANES), BF16),
            pltpu.VMEM((chans, lats, pad, LANES), BF16),
            pltpu.VMEM((chans, lats, pad, LANES), BF16),
            pltpu.VMEM((owners, pad, LANES), BF16),
            pltpu.VMEM((quads, part, channels), F32),
            pltpu.VMEM((quads, part, channels), BF16),
            pltpu.VMEM((quads - 1, part, channels), BF16),
            pltpu.VMEM((lats, piece, channels), F32),
            pltpu.VMEM((lats, piece, channels), BF16),
            pltpu.VMEM((lats - 1, piece, channels), BF16),
            dma((len(operands),)),
            dma((1 + quads,)),
            dma((2, 1)),
            dma((2, owners - 1)),
            dma((2, owners - 1)),
            dma((2, quads - 1)),
            dma((2, lats - 1)),
            dma((2, lats - 1)),
            dma((2, quads - 1, lats)),
        ],
        compiler_params=pltpu.CompilerParams(
            collective_id=0, has_side_effects=True, vmem_limit_bytes=60 << 20
        ),
    )(*operands)
    result, weight = pl.pallas_call(
        copy_kernel,
        out_shape=(
            jax.ShapeDtypeStruct(result.shape, BF16),
            jax.ShapeDtypeStruct(weight.shape, F32),
        ),
        in_specs=[pl.BlockSpec(memory_space=pltpu.HBM)] * 2,
        out_specs=(pl.BlockSpec(memory_space=pltpu.HBM),) * 2,
        scratch_shapes=[dma((2,))],
        compiler_params=pltpu.CompilerParams(vmem_limit_bytes=60 << 20),
    )(result, weight)
    return result.reshape(grad_out.shape), weight


def fits(mesh, rows, lon, channels):
    lats, chans, members = (mesh.shape[axis] for axis in ("lat", "chan", "ens"))
    return (
        members == 2 and lats * chans <= 8 and rows * lon <= 512
        and lon % 16 == 0 and rows % 2 == 0
        and channels // mesh.shape["chan"] == LANES + LANES // 2
        and channels % (members * chans * lats * 8) == 0
    )


def solution(mesh):
    placed = (
        P(("grp", "ens"), "lat", None, "chan"),
        P(("grp", "ens"), "lat", None, "chan"),
        P(("grp", "ens"), ("lat", "chan"), None, None, None),
        P(("lat", "chan"), None, "ens"),
        P(),
    )

    def local(grad_out, *rest):
        rows, lon, cols = grad_out.shape[1:]
        small = fits(mesh, rows, lon, cols * mesh.shape["chan"])
        return (fused if small else on_device)(grad_out, *rest)

    return jax.shard_map(
        local,
        mesh=mesh,
        in_specs=placed,
        out_specs=(P(("grp", "ens"), "lat", None, "chan"), P("grp", None)),
        check_vma=False,
    )
```

```python
import math

import jax
import jax.numpy as jnp
import numpy as np
from jax import lax
from jax.experimental import pallas as pl
from jax.experimental.pallas import tpu as pltpu
from jax.sharding import PartitionSpec as P


def fourier_table(lon_count, mode_count):
    longitude = jnp.arange(lon_count, dtype=jnp.int32)[:, None]
    wavenumber = jnp.arange(mode_count, dtype=jnp.int32)[None, :]
    product_index = longitude * wavenumber % lon_count
    angles = 2.0 * math.pi / lon_count * product_index.astype(jnp.float32)
    factor = math.sqrt(2.0 / lon_count)
    stacked = jnp.stack([jnp.cos(angles), -jnp.sin(angles)], axis=2) * factor
    return stacked.reshape(lon_count, 2 * mode_count).astype(jnp.bfloat16)


def silu_backward(cotangent, preact):
    values = preact.astype(jnp.float32)
    gate_value = jax.nn.sigmoid(values)
    return (
        cotangent.astype(jnp.float32) * gate_value * (1.0 + values * (1.0 - gate_value))
    ).astype(jnp.bfloat16)


def on_device(grad_out, pre_act, coeffs, legendre, mixing):
    lat_rows = grad_out.shape[1]
    lon_count = grad_out.shape[2]
    chan_cols = grad_out.shape[3]
    mode_count = lon_count // 2
    lat_devices = lax.axis_size("lat")
    chan_count = lax.axis_size("chan")
    members = lax.axis_size("ens")
    lat_count = lat_rows * lat_devices
    channels = chan_cols * chan_count
    mode_width = 2 * mode_count // (lat_devices * chan_count)
    local_modes = mode_width // 2
    fourier = fourier_table(lon_count, mode_count)
    scaled = silu_backward(grad_out[0], pre_act[0])
    spectral = jnp.einsum(
        "nk,anc->akc", fourier, scaled, preferred_element_type=jnp.float32
    ).astype(jnp.bfloat16)
    exchanged = lax.all_to_all(
        lax.all_to_all(spectral, "lat", split_axis=1, concat_axis=0, tiled=True),
        "chan",
        split_axis=1,
        concat_axis=2,
        tiled=True,
    )
    spectral_modes = exchanged.reshape(lat_count, local_modes, 2, channels)
    legendre_full = lax.all_gather(legendre, "ens", axis=2, tiled=True)
    coef_grad = jnp.einsum(
        "mla,amrc->mlrc", legendre_full, spectral_modes, preferred_element_type=jnp.float32
    ).astype(jnp.bfloat16)
    stored = coeffs[0].reshape(-1, channels)
    flat_grad = coef_grad.reshape(-1, channels)
    weight_grad = lax.dot_general(
        stored, flat_grad, (((0,), (0,)), ((), ())), preferred_element_type=jnp.float32
    )
    weight_grad = weight_grad * (1.0 / (members * mode_count))
    weight_grad = lax.psum(weight_grad, ("lat", "chan", "ens"))
    mixed_grad = lax.dot_general(
        coef_grad, mixing, (((3,), (1,)), ((), ())), preferred_element_type=jnp.float32
    ).astype(jnp.bfloat16)
    returned = jnp.einsum(
        "mla,mlrc->amrc", legendre_full, mixed_grad, preferred_element_type=jnp.float32
    ).astype(jnp.bfloat16)
    shaped = returned.reshape(lat_count, 1, mode_width, channels)
    received = lax.all_to_all(
        lax.all_to_all(shaped, "lat", split_axis=0, concat_axis=1, tiled=True),
        "chan",
        split_axis=3,
        concat_axis=2,
        tiled=True,
    )
    row_coeffs = received.reshape(lat_rows, 2 * mode_count, chan_cols)
    spatial = jnp.einsum("nk,akc->anc", fourier, row_coeffs, preferred_element_type=jnp.float32)
    result = (grad_out[0].astype(jnp.float32) + spatial).astype(jnp.bfloat16)
    return (result[None], weight_grad)

MESH = pl.DeviceIdType.MESH
BF16 = jnp.bfloat16
F32 = jnp.float32


def dot(a, b, dims=((1,), (0,))):
    return lax.dot_general(a, b, (dims, ((), ())), preferred_element_type=F32)


LANES = 128


def slots(rows, width):
    whole = [(a, a, k) for a in range(rows) for k in range(width)]
    paired = [(a, a + 1, k) for a in range(0, rows, 2) for k in range(width)]
    return whole, paired


def padded(rows, width):
    return -(-(rows + rows // 2) * width // 16) * 16


def tables(rows, lon, lats, chans, members, modes, degrees):
    owners = lats * chans
    width = 2 * modes
    pad = padded(rows, width)
    n = np.arange(lon)[:, None]
    m = np.arange(lon // 2)[None, :]
    angles = np.float32(2.0 * math.pi / lon) * (n * m % lon).astype(np.float32)
    table = np.stack([np.cos(angles), -np.sin(angles)], axis=2).reshape(lon, lon)
    table = (table * np.float32(math.sqrt(2.0 / lon))).astype(np.float32)
    groups = rows + rows // 2
    inverse = np.zeros((groups, lon, owners, pad), np.float32)
    for g in range(groups):
        for d in range(owners):
            inverse[g, :, d, g * width:(g + 1) * width] = table[:, d * width:(d + 1) * width]
    inverse = inverse.reshape(groups * lon, owners * pad)
    whole, paired = slots(rows, width)
    lat_of = np.full((3, lats, pad), -1)
    key_of = np.full((3, lats, pad), -1)
    for z in range(lats):
        for i, (even, odd, k) in enumerate(whole + paired):
            if i < len(whole):
                lat_of[0, z, i], key_of[0, z, i] = z * rows + even, k
            else:
                lat_of[1, z, i], key_of[1, z, i] = z * rows + even, k
                lat_of[2, z, i], key_of[2, z, i] = z * rows + odd, k
    lat_of, key_of = lat_of.reshape(-1), key_of.reshape(-1)
    held = rows * lats // members
    select = (lat_of[None, :] == np.arange(members * held)[:, None]).astype(np.float32)
    select = select.reshape(members, held, -1)
    row = np.arange(modes * degrees * 2)
    spread = (row[:, None] // 2 == np.arange(modes * degrees)[None, :]).astype(np.float32)
    row_key = row // (2 * degrees) * 2 + row % 2
    mask = (row_key[:, None] == key_of[None, :]).astype(np.float32)
    cast = lambda x: jnp.asarray(np.ascontiguousarray(x), BF16)
    return (
        cast(inverse.T), cast(inverse), cast(select), cast(select.transpose(0, 2, 1)),
        cast(spread), cast(spread.T), cast(mask), cast(mask.T),
    )


def fused_kernel(
    lats, chans, members, lon,
    grad_hbm, pre_hbm, coeffs_hbm, leg_hbm, mix_hbm,
    fwd_hbm, inv_hbm, sel_hbm, selt_hbm, spread_hbm, spreadt_hbm, mask_hbm, maskt_hbm,
    out_hbm, full_hbm,
    out_ref, full_ref,
    grad_ref, pre_ref, coeffs_ref, leg_ref, mix_ref,
    fwd_ref, inv_ref, sel_ref, selt_ref, spread_ref, spreadt_ref, mask_ref, maskt_ref,
    stored, lbuf, sbuf, rbuf, sbuf2, rbuf2, w1s, w1r, w2own, w2s, w2r,
    isem, osem, lsem, esem, fsem, r1sem, r2sem, g1sem, g2sem,
):
    z, c, x = lax.axis_index("lat"), lax.axis_index("chan"), lax.axis_index("ens")
    owners, quads = lats * chans, members * chans
    me, quad = z * chans + c, x * chans + c
    pad, cols, blocks = rbuf.shape[2], grad_ref.shape[1], lats * rbuf.shape[2]

    def owner_peer(p):
        q = lax.rem(me + p, owners)
        return q, q // chans, lax.rem(q, chans)

    def quad_peer(p):
        q = lax.rem(quad + p, quads)
        return q, q // chans, lax.rem(q, chans)

    sources = (
        pre_hbm, grad_hbm, fwd_hbm, leg_hbm, sel_hbm, selt_hbm, spread_hbm, spreadt_hbm,
        mask_hbm, maskt_hbm, coeffs_hbm, mix_hbm, inv_hbm,
    )
    targets = (
        pre_ref, grad_ref, fwd_ref, leg_ref, sel_ref, selt_ref, spread_ref, spreadt_ref,
        mask_ref, maskt_ref, coeffs_ref, mix_ref, inv_ref,
    )
    loads = [
        pltpu.make_async_copy(source, target, isem.at[i])
        for i, (source, target) in enumerate(zip(sources, targets))
    ]
    for load in loads:
        load.start()
    barrier = pltpu.get_barrier_semaphore()
    for p in range(1, owners):
        _, pz, pc = owner_peer(p)
        pl.semaphore_signal(barrier, inc=1, device_id={"lat": pz, "chan": pc}, device_id_type=MESH)
    for p in range(1, members):
        for pc in range(chans):
            target = {"ens": lax.rem(x + p, members), "chan": pc}
            pl.semaphore_signal(barrier, inc=1, device_id=target, device_id_type=MESH)

    for load in loads[:4]:
        load.wait()
    values = pre_ref[...].astype(F32)
    gate = jax.nn.sigmoid(values)
    scaled = grad_ref[...].astype(F32) * gate * (1.0 + values * (1.0 - gate))
    points, half = scaled.shape[0], LANES // 2
    tail = scaled[:, LANES:].reshape(-1, 2, lon, half)
    paired = jnp.concatenate([tail[:, 0], tail[:, 1]], axis=-1).reshape(-1, LANES)
    packed = jnp.concatenate([scaled[:, :LANES], paired], axis=0).astype(BF16)
    sbuf[...] = dot(fwd_ref[...], packed).astype(BF16).reshape(owners, pad, LANES)

    pl.semaphore_wait(barrier, owners - 1 + (members - 1) * chans)

    def remote(src, dst, sems, target):
        return pltpu.make_async_remote_copy(
            src_ref=src, dst_ref=dst, send_sem=sems[0], recv_sem=sems[1],
            device_id=target, device_id_type=MESH,
        )

    def pair(sem, *index):
        return sem.at[(0,) + index], sem.at[(1,) + index]

    legs = remote(leg_ref, lbuf, pair(lsem, 0), {"ens": lax.rem(x + 1, members)})
    legs.start()
    started = [legs]
    first = []
    for p in range(1, owners):
        q, pz, pc = owner_peer(p)
        copy = remote(sbuf.at[q], rbuf.at[c, z], pair(esem, p - 1), {"lat": pz, "chan": pc})
        copy.start()
        first.append(copy)
    started += first
    for load in loads[4:]:
        load.wait()
    rbuf[c, z] = sbuf[me]
    legs.wait_recv()
    other = lax.rem(x + 1, members)
    modes, degrees = leg_ref.shape[0], leg_ref.shape[2]
    by_lat, synthesis = [], 0.0
    for m in range(modes):
        mine, theirs = leg_ref[m], lbuf[m]
        down = ((0,), (0,))
        by_lat.append(dot(mine, sel_ref[x], down) + dot(theirs, sel_ref[other], down))
        by_row = dot(selt_ref[x], mine) + dot(selt_ref[other], theirs)
        rows = spreadt_ref[m * degrees:(m + 1) * degrees, :]
        synthesis = synthesis + dot(by_row.astype(BF16), rows)
    by_lat = jnp.concatenate(by_lat, axis=0).astype(BF16)
    analysis = (dot(spread_ref[...], by_lat) * mask_ref[...].astype(F32)).astype(BF16)
    synthesis = (synthesis * maskt_ref[...].astype(F32)).astype(BF16)
    across = ((1,), (1,))
    flat = coeffs_ref[...].reshape(stored.shape[::-1])
    stored[...] = flat.astype(F32).T.astype(BF16)

    for copy in first:
        copy.wait_recv()
    halves = []
    for h in range(chans):
        held = rbuf[h].reshape(blocks, LANES)
        wide, even, odd = (dot(analysis[:, v * blocks:(v + 1) * blocks], held) for v in range(3))
        halves += [wide, even[:, :half] + odd[:, half:]]
    coef = jnp.concatenate(halves, axis=1).astype(BF16)

    part = w1s.shape[1]

    def weight(q):
        return dot(stored[pl.ds(pl.multiple_of(q * part, part), part), :], coef)

    reduce1 = []
    for p in range(quads - 1, 0, -1):
        q, px, pc = quad_peer(p)
        w1s[q] = weight(q).astype(BF16)
        copy = remote(w1s.at[q], w1r.at[p - 1], pair(r1sem, p - 1), {"ens": px, "chan": pc})
        copy.start()
        reduce1.append(copy)
    started += reduce1
    own = weight(quad)

    for h in range(chans):
        mixed = dot(coef, mix_ref[h * cols:(h + 1) * cols, :], across)
        rest = mixed[:, LANES:]
        none = jnp.zeros_like(rest)
        sides = (
            mixed[:, :LANES],
            jnp.concatenate([rest, none], axis=1),
            jnp.concatenate([none, rest], axis=1),
        )
        returned = sum(
            dot(synthesis[v * blocks:(v + 1) * blocks], side.astype(BF16))
            for v, side in enumerate(sides)
        )
        sbuf2[h] = returned.astype(BF16).reshape(lats, pad, LANES)
    second = []
    for p in range(1, owners):
        q, pz, pc = owner_peer(p)
        copy = remote(sbuf2.at[pc, pz], rbuf2.at[me], pair(fsem, p - 1), {"lat": pz, "chan": pc})
        copy.start()
        second.append(copy)
    started += second
    rbuf2[me] = sbuf2[c, z]

    total = own
    for p, copy in zip(range(quads - 1, 0, -1), reduce1):
        copy.wait_recv()
        total = total + w1r[p - 1].astype(F32)
    total = total.reshape(w2own.shape)
    w2own[...] = total
    w2s[...] = total.astype(BF16)
    reduce2 = []
    for p in range(1, lats):
        pz = lax.rem(z + p, lats)
        copy = remote(w2s.at[pz], w2r.at[p - 1], pair(r2sem, p - 1), {"lat": pz})
        copy.start()
        reduce2.append(copy)
    started += reduce2

    for copy in second:
        copy.wait_recv()
    spatial = dot(inv_ref[...], rbuf2[...].reshape(owners * pad, LANES))
    pairs = spatial[points:].reshape(-1, 1, lon, LANES)
    rest = jnp.concatenate([pairs[..., :half], pairs[..., half:]], axis=1).reshape(points, half)
    spatial = jnp.concatenate([spatial[:points], rest], axis=1)
    out_ref[...] = (grad_ref[...].astype(F32) + spatial).astype(BF16)
    stores = [pltpu.make_async_copy(out_ref, out_hbm, osem.at[0])]
    stores[0].start()

    piece = w2own[z]
    for p, copy in enumerate(reduce2):
        copy.wait_recv()
        piece = piece + w2r[p].astype(F32)
    full_ref[quad, z] = piece.astype(BF16)
    gather1 = []
    for p in range(1, lats):
        pz = lax.rem(z + p, lats)
        copy = remote(full_ref.at[quad, z], full_ref.at[quad, z], pair(g1sem, p - 1), {"lat": pz})
        copy.start()
        gather1.append(copy)
    started += gather1
    gather2 = []
    for s in range(lats):
        if s > 0:
            gather1[s - 1].wait_recv()
        source = lax.rem(z + lats - s, lats)
        for p in range(1, quads):
            q, px, pc = quad_peer(p)
            block = full_ref.at[quad, source]
            copy = remote(block, block, pair(g2sem, p - 1, s), {"ens": px, "chan": pc})
            copy.start()
            gather2.append(copy)
    for p in range(quads):
        if p > 0:
            for s in range(lats):
                gather2[s * (quads - 1) + p - 1].wait_recv()
        block = lax.rem(quad + quads - p, quads)
        store = pltpu.make_async_copy(full_ref.at[block], full_hbm.at[block], osem.at[1 + p])
        store.start()
        stores.append(store)
    started += gather2
    for copy in started:
        copy.wait_send()
    for store in stores:
        store.wait()


def fused(grad_out, pre_act, coeffs, legendre, mixing):
    rows, lon, cols = grad_out.shape[1:]
    lats, chans = lax.axis_size("lat"), lax.axis_size("chan")
    members = lax.axis_size("ens")
    modes, degrees, held = legendre.shape
    owners, quads, channels = lats * chans, members * chans, cols * chans
    pad = padded(rows, 2 * modes)
    part, piece = channels // quads, channels // quads // lats
    constants = tables(rows, lon, lats, chans, members, modes, degrees)
    dma = pltpu.SemaphoreType.DMA

    def kernel(*refs):
        fused_kernel(lats, chans, members, lon, *refs)

    operands = (
        grad_out.reshape(rows * lon, cols),
        pre_act.reshape(rows * lon, cols),
        coeffs.reshape(modes * degrees, 2, channels),
        legendre.transpose(0, 2, 1),
        mixing,
        *constants,
    )
    result, weight = pl.pallas_call(
        kernel,
        out_shape=(
            jax.ShapeDtypeStruct((rows * lon, cols), BF16),
            jax.ShapeDtypeStruct((quads, lats, piece, channels), BF16),
        ),
        in_specs=[pl.BlockSpec(memory_space=pltpu.HBM)] * 13,
        out_specs=(pl.BlockSpec(memory_space=pltpu.HBM),) * 2,
        scratch_shapes=[
            pltpu.VMEM((rows * lon, cols), BF16),
            pltpu.VMEM((quads, lats, piece, channels), BF16),
            *[pltpu.VMEM(operand.shape, BF16) for operand in operands],
            pltpu.VMEM((channels, modes * degrees * 2), BF16),
            pltpu.VMEM((modes, held, degrees), BF16),
            pltpu.VMEM((owners, pad, LANES), BF16),
            pltpu.VMEM((chans, lats, pad, LANES), BF16),
            pltpu.VMEM((chans, lats, pad, LANES), BF16),
            pltpu.VMEM((owners, pad, LANES), BF16),
            pltpu.VMEM((quads, part, channels), BF16),
            pltpu.VMEM((quads - 1, part, channels), BF16),
            pltpu.VMEM((lats, piece, channels), F32),
            pltpu.VMEM((lats, piece, channels), BF16),
            pltpu.VMEM((lats - 1, piece, channels), BF16),
            dma((len(operands),)),
            dma((1 + quads,)),
            dma((2, 1)),
            dma((2, owners - 1)),
            dma((2, owners - 1)),
            dma((2, quads - 1)),
            dma((2, lats - 1)),
            dma((2, lats - 1)),
            dma((2, quads - 1, lats)),
        ],
        compiler_params=pltpu.CompilerParams(
            collective_id=0, has_side_effects=True, vmem_limit_bytes=60 << 20
        ),
    )(*operands)
    weight = weight.astype(F32).reshape(channels, channels) * (1.0 / (members * lon // 2))
    return result.reshape(grad_out.shape), weight


def fits(mesh, rows, lon, channels):
    lats, chans, members = (mesh.shape[axis] for axis in ("lat", "chan", "ens"))
    return (
        members == 2 and lats * chans <= 8 and rows * lon <= 512
        and lon % 16 == 0 and rows % 2 == 0
        and channels // mesh.shape["chan"] == LANES + LANES // 2
        and channels % (members * chans * lats * 8) == 0
    )


def solution(mesh):
    placed = (
        P(("grp", "ens"), "lat", None, "chan"),
        P(("grp", "ens"), "lat", None, "chan"),
        P(("grp", "ens"), ("lat", "chan"), None, None, None),
        P(("lat", "chan"), None, "ens"),
        P(),
    )

    def local(grad_out, *rest):
        rows, lon, cols = grad_out.shape[1:]
        small = fits(mesh, rows, lon, cols * mesh.shape["chan"])
        return (fused if small else on_device)(grad_out, *rest)

    return jax.shard_map(
        local,
        mesh=mesh,
        in_specs=placed,
        out_specs=(P(("grp", "ens"), "lat", None, "chan"), P("grp", None)),
        check_vma=False,
    )
```

```python
import math

import jax
import jax.numpy as jnp
import numpy as np
from jax import lax
from jax.experimental import pallas as pl
from jax.experimental.pallas import tpu as pltpu
from jax.sharding import PartitionSpec as P


def fourier_table(lon_count, mode_count):
    longitude = jnp.arange(lon_count, dtype=jnp.int32)[:, None]
    wavenumber = jnp.arange(mode_count, dtype=jnp.int32)[None, :]
    product_index = longitude * wavenumber % lon_count
    angles = 2.0 * math.pi / lon_count * product_index.astype(jnp.float32)
    factor = math.sqrt(2.0 / lon_count)
    stacked = jnp.stack([jnp.cos(angles), -jnp.sin(angles)], axis=2) * factor
    return stacked.reshape(lon_count, 2 * mode_count).astype(jnp.bfloat16)


def silu_backward(cotangent, preact):
    values = preact.astype(jnp.float32)
    gate_value = jax.nn.sigmoid(values)
    return (
        cotangent.astype(jnp.float32) * gate_value * (1.0 + values * (1.0 - gate_value))
    ).astype(jnp.bfloat16)


def on_device(grad_out, pre_act, coeffs, legendre, mixing):
    lat_rows = grad_out.shape[1]
    lon_count = grad_out.shape[2]
    chan_cols = grad_out.shape[3]
    mode_count = lon_count // 2
    lat_devices = lax.axis_size("lat")
    chan_count = lax.axis_size("chan")
    members = lax.axis_size("ens")
    lat_count = lat_rows * lat_devices
    channels = chan_cols * chan_count
    mode_width = 2 * mode_count // (lat_devices * chan_count)
    local_modes = mode_width // 2
    fourier = fourier_table(lon_count, mode_count)
    scaled = silu_backward(grad_out[0], pre_act[0])
    spectral = jnp.einsum(
        "nk,anc->akc", fourier, scaled, preferred_element_type=jnp.float32
    ).astype(jnp.bfloat16)
    exchanged = lax.all_to_all(
        lax.all_to_all(spectral, "lat", split_axis=1, concat_axis=0, tiled=True),
        "chan",
        split_axis=1,
        concat_axis=2,
        tiled=True,
    )
    spectral_modes = exchanged.reshape(lat_count, local_modes, 2, channels)
    legendre_full = lax.all_gather(legendre, "ens", axis=2, tiled=True)
    coef_grad = jnp.einsum(
        "mla,amrc->mlrc", legendre_full, spectral_modes, preferred_element_type=jnp.float32
    ).astype(jnp.bfloat16)
    stored = coeffs[0].reshape(-1, channels)
    flat_grad = coef_grad.reshape(-1, channels)
    weight_grad = lax.dot_general(
        stored, flat_grad, (((0,), (0,)), ((), ())), preferred_element_type=jnp.float32
    )
    weight_grad = weight_grad * (1.0 / (members * mode_count))
    weight_grad = lax.psum(weight_grad, ("lat", "chan", "ens"))
    mixed_grad = lax.dot_general(
        coef_grad, mixing, (((3,), (1,)), ((), ())), preferred_element_type=jnp.float32
    ).astype(jnp.bfloat16)
    returned = jnp.einsum(
        "mla,mlrc->amrc", legendre_full, mixed_grad, preferred_element_type=jnp.float32
    ).astype(jnp.bfloat16)
    shaped = returned.reshape(lat_count, 1, mode_width, channels)
    received = lax.all_to_all(
        lax.all_to_all(shaped, "lat", split_axis=0, concat_axis=1, tiled=True),
        "chan",
        split_axis=3,
        concat_axis=2,
        tiled=True,
    )
    row_coeffs = received.reshape(lat_rows, 2 * mode_count, chan_cols)
    spatial = jnp.einsum("nk,akc->anc", fourier, row_coeffs, preferred_element_type=jnp.float32)
    result = (grad_out[0].astype(jnp.float32) + spatial).astype(jnp.bfloat16)
    return (result[None], weight_grad)

MESH = pl.DeviceIdType.MESH
BF16 = jnp.bfloat16
F32 = jnp.float32


def dot(a, b, dims=((1,), (0,))):
    return lax.dot_general(a, b, (dims, ((), ())), preferred_element_type=F32)


LANES = 128


def slots(rows, width):
    whole = [(a, a, k) for a in range(rows) for k in range(width)]
    paired = [(a, a + 1, k) for a in range(0, rows, 2) for k in range(width)]
    return whole, paired


def padded(rows, width):
    return -(-(rows + rows // 2) * width // 16) * 16


def tables(rows, lon, lats, chans, members, modes, degrees):
    owners = lats * chans
    width = 2 * modes
    pad = padded(rows, width)
    n = np.arange(lon)[:, None]
    m = np.arange(lon // 2)[None, :]
    angles = np.float32(2.0 * math.pi / lon) * (n * m % lon).astype(np.float32)
    table = np.stack([np.cos(angles), -np.sin(angles)], axis=2).reshape(lon, lon)
    table = (table * np.float32(math.sqrt(2.0 / lon))).astype(np.float32)
    groups = rows + rows // 2
    inverse = np.zeros((groups, lon, owners, pad), np.float32)
    for g in range(groups):
        for d in range(owners):
            inverse[g, :, d, g * width:(g + 1) * width] = table[:, d * width:(d + 1) * width]
    inverse = inverse.reshape(groups * lon, owners * pad)
    whole, paired = slots(rows, width)
    lat_of = np.full((3, lats, pad), -1)
    key_of = np.full((3, lats, pad), -1)
    for z in range(lats):
        for i, (even, odd, k) in enumerate(whole + paired):
            if i < len(whole):
                lat_of[0, z, i], key_of[0, z, i] = z * rows + even, k
            else:
                lat_of[1, z, i], key_of[1, z, i] = z * rows + even, k
                lat_of[2, z, i], key_of[2, z, i] = z * rows + odd, k
    lat_of, key_of = lat_of.reshape(-1), key_of.reshape(-1)
    held = rows * lats // members
    select = (lat_of[None, :] == np.arange(members * held)[:, None]).astype(np.float32)
    select = select.reshape(members, held, -1)
    row = np.arange(modes * degrees * 2)
    spread = (row[:, None] // 2 == np.arange(modes * degrees)[None, :]).astype(np.float32)
    row_key = row // (2 * degrees) * 2 + row % 2
    mask = (row_key[:, None] == key_of[None, :]).astype(np.float32)
    cast = lambda x: jnp.asarray(np.ascontiguousarray(x), BF16)
    return (
        cast(inverse.T), cast(inverse), cast(select), cast(select.transpose(0, 2, 1)),
        cast(spread), cast(spread.T), cast(mask), cast(mask.T),
    )


def fused_kernel(
    lats, chans, members, lon,
    grad_hbm, pre_hbm, coeffs_hbm, leg_hbm, mix_hbm,
    fwd_hbm, inv_hbm, sel_hbm, selt_hbm, spread_hbm, spreadt_hbm, mask_hbm, maskt_hbm,
    out_hbm, full_hbm,
    out_ref, full_ref,
    grad_ref, pre_ref, coeffs_ref, leg_ref, mix_ref,
    fwd_ref, inv_ref, sel_ref, selt_ref, spread_ref, spreadt_ref, mask_ref, maskt_ref,
    stored, lbuf, sbuf, rbuf, sbuf2, rbuf2, w1s, w1r, w2own, w2s, w2r,
    isem, osem, lsem, esem, fsem, r1sem, r2sem, g1sem, g2sem,
):
    z, c, x = lax.axis_index("lat"), lax.axis_index("chan"), lax.axis_index("ens")
    owners, quads = lats * chans, members * chans
    me, quad = z * chans + c, x * chans + c
    pad, cols, blocks = rbuf.shape[2], grad_ref.shape[1], lats * rbuf.shape[2]

    def owner_peer(p):
        q = lax.rem(me + p, owners)
        return q, q // chans, lax.rem(q, chans)

    def quad_peer(p):
        q = lax.rem(quad + p, quads)
        return q, q // chans, lax.rem(q, chans)

    sources = (
        pre_hbm, grad_hbm, fwd_hbm, leg_hbm, sel_hbm, selt_hbm, spread_hbm, spreadt_hbm,
        mask_hbm, maskt_hbm, coeffs_hbm, mix_hbm, inv_hbm,
    )
    targets = (
        pre_ref, grad_ref, fwd_ref, leg_ref, sel_ref, selt_ref, spread_ref, spreadt_ref,
        mask_ref, maskt_ref, coeffs_ref, mix_ref, inv_ref,
    )
    loads = [
        pltpu.make_async_copy(source, target, isem.at[i])
        for i, (source, target) in enumerate(zip(sources, targets))
    ]
    for load in loads:
        load.start()
    barrier = pltpu.get_barrier_semaphore()
    for p in range(1, owners):
        _, pz, pc = owner_peer(p)
        pl.semaphore_signal(barrier, inc=1, device_id={"lat": pz, "chan": pc}, device_id_type=MESH)
    for p in range(1, members):
        for pc in range(chans):
            target = {"ens": lax.rem(x + p, members), "chan": pc}
            pl.semaphore_signal(barrier, inc=1, device_id=target, device_id_type=MESH)

    for load in loads[:4]:
        load.wait()
    values = pre_ref[...].astype(F32)
    gate = jax.nn.sigmoid(values)
    scaled = grad_ref[...].astype(F32) * gate * (1.0 + values * (1.0 - gate))
    points, half = scaled.shape[0], LANES // 2
    tail = scaled[:, LANES:].reshape(-1, 2, lon, half)
    paired = jnp.concatenate([tail[:, 0], tail[:, 1]], axis=-1).reshape(-1, LANES)
    packed = jnp.concatenate([scaled[:, :LANES], paired], axis=0).astype(BF16)
    sbuf[...] = dot(fwd_ref[...], packed).astype(BF16).reshape(owners, pad, LANES)

    pl.semaphore_wait(barrier, owners - 1 + (members - 1) * chans)

    def remote(src, dst, sems, target):
        return pltpu.make_async_remote_copy(
            src_ref=src, dst_ref=dst, send_sem=sems[0], recv_sem=sems[1],
            device_id=target, device_id_type=MESH,
        )

    def pair(sem, *index):
        return sem.at[(0,) + index], sem.at[(1,) + index]

    legs = remote(leg_ref, lbuf, pair(lsem, 0), {"ens": lax.rem(x + 1, members)})
    legs.start()
    started = [legs]
    first = []
    for p in sorted(range(1, owners), key=lambda p: abs(p - owners // 2)):
        q, pz, pc = owner_peer(p)
        copy = remote(sbuf.at[q], rbuf.at[c, z], pair(esem, p - 1), {"lat": pz, "chan": pc})
        copy.start()
        first.append(copy)
    started += first
    for load in loads[4:]:
        load.wait()
    rbuf[c, z] = sbuf[me]
    legs.wait_recv()
    other = lax.rem(x + 1, members)
    modes, degrees = leg_ref.shape[0], leg_ref.shape[2]
    by_lat, synthesis = [], 0.0
    for m in range(modes):
        mine, theirs = leg_ref[m], lbuf[m]
        down = ((0,), (0,))
        by_lat.append(dot(mine, sel_ref[x], down) + dot(theirs, sel_ref[other], down))
        by_row = dot(selt_ref[x], mine) + dot(selt_ref[other], theirs)
        rows = spreadt_ref[m * degrees:(m + 1) * degrees, :]
        synthesis = synthesis + dot(by_row.astype(BF16), rows)
    by_lat = jnp.concatenate(by_lat, axis=0).astype(BF16)
    analysis = (dot(spread_ref[...], by_lat) * mask_ref[...].astype(F32)).astype(BF16)
    synthesis = (synthesis * maskt_ref[...].astype(F32)).astype(BF16)
    across = ((1,), (1,))
    flat = coeffs_ref[...].reshape(stored.shape[::-1])
    stored[...] = flat.astype(F32).T.astype(BF16)

    for copy in first:
        copy.wait_recv()
    halves = []
    for h in range(chans):
        held = rbuf[h].reshape(blocks, LANES)
        wide, even, odd = (dot(analysis[:, v * blocks:(v + 1) * blocks], held) for v in range(3))
        halves += [wide, even[:, :half] + odd[:, half:]]
    coef = jnp.concatenate(halves, axis=1).astype(BF16)

    part = w1s.shape[1]

    def weight(q):
        return dot(stored[pl.ds(pl.multiple_of(q * part, part), part), :], coef)

    reduce1 = []
    for p in range(quads - 1, 0, -1):
        q, px, pc = quad_peer(p)
        w1s[q] = weight(q).astype(BF16)
        copy = remote(w1s.at[q], w1r.at[p - 1], pair(r1sem, p - 1), {"ens": px, "chan": pc})
        copy.start()
        reduce1.append(copy)
    started += reduce1
    own = weight(quad)

    for h in range(chans):
        mixed = dot(coef, mix_ref[h * cols:(h + 1) * cols, :], across)
        rest = mixed[:, LANES:]
        none = jnp.zeros_like(rest)
        sides = (
            mixed[:, :LANES],
            jnp.concatenate([rest, none], axis=1),
            jnp.concatenate([none, rest], axis=1),
        )
        returned = sum(
            dot(synthesis[v * blocks:(v + 1) * blocks], side.astype(BF16))
            for v, side in enumerate(sides)
        )
        sbuf2[h] = returned.astype(BF16).reshape(lats, pad, LANES)
    second = []
    for p in sorted(range(1, owners), key=lambda p: abs(p - owners // 2)):
        q, pz, pc = owner_peer(p)
        copy = remote(sbuf2.at[pc, pz], rbuf2.at[me], pair(fsem, p - 1), {"lat": pz, "chan": pc})
        copy.start()
        second.append(copy)
    started += second
    rbuf2[me] = sbuf2[c, z]

    total = own
    for p, copy in zip(range(quads - 1, 0, -1), reduce1):
        copy.wait_recv()
        total = total + w1r[p - 1].astype(F32)
    total = total.reshape(w2own.shape)
    w2own[...] = total
    w2s[...] = total.astype(BF16)
    reduce2 = []
    for p in range(1, lats):
        pz = lax.rem(z + p, lats)
        copy = remote(w2s.at[pz], w2r.at[p - 1], pair(r2sem, p - 1), {"lat": pz})
        copy.start()
        reduce2.append(copy)
    started += reduce2

    def finish():
        for copy in second:
            copy.wait_recv()
        spatial = dot(inv_ref[...], rbuf2[...].reshape(owners * pad, LANES))
        pairs = spatial[points:].reshape(-1, 1, lon, LANES)
        rest = jnp.concatenate([pairs[..., :half], pairs[..., half:]], axis=1).reshape(points, half)
        spatial = jnp.concatenate([spatial[:points], rest], axis=1)
        out_ref[...] = (grad_ref[...].astype(F32) + spatial).astype(BF16)
        stores = [pltpu.make_async_copy(out_ref, out_hbm, osem.at[0])]
        stores[0].start()
        return stores

    piece = w2own[z]
    for p, copy in enumerate(reduce2):
        copy.wait_recv()
        piece = piece + w2r[p].astype(F32)
    full_ref[quad, z] = piece.astype(BF16)
    gather1 = []
    for p in range(1, lats):
        pz = lax.rem(z + p, lats)
        copy = remote(full_ref.at[quad, z], full_ref.at[quad, z], pair(g1sem, p - 1), {"lat": pz})
        copy.start()
        gather1.append(copy)
    started += gather1
    gather2 = []
    for s in range(lats):
        if s == 1:
            stores = finish()
        if s > 0:
            gather1[s - 1].wait_recv()
        source = lax.rem(z + lats - s, lats)
        for p in range(1, quads):
            q, px, pc = quad_peer(p)
            block = full_ref.at[quad, source]
            copy = remote(block, block, pair(g2sem, p - 1, s), {"ens": px, "chan": pc})
            copy.start()
            gather2.append(copy)
    for p in range(quads):
        if p > 0:
            for s in range(lats):
                gather2[s * (quads - 1) + p - 1].wait_recv()
        block = lax.rem(quad + quads - p, quads)
        store = pltpu.make_async_copy(full_ref.at[block], full_hbm.at[block], osem.at[1 + p])
        store.start()
        stores.append(store)
    started += gather2
    for copy in started:
        copy.wait_send()
    for store in stores:
        store.wait()


def fused(grad_out, pre_act, coeffs, legendre, mixing):
    rows, lon, cols = grad_out.shape[1:]
    lats, chans = lax.axis_size("lat"), lax.axis_size("chan")
    members = lax.axis_size("ens")
    modes, degrees, held = legendre.shape
    owners, quads, channels = lats * chans, members * chans, cols * chans
    pad = padded(rows, 2 * modes)
    part, piece = channels // quads, channels // quads // lats
    constants = tables(rows, lon, lats, chans, members, modes, degrees)
    dma = pltpu.SemaphoreType.DMA

    def kernel(*refs):
        fused_kernel(lats, chans, members, lon, *refs)

    operands = (
        grad_out.reshape(rows * lon, cols),
        pre_act.reshape(rows * lon, cols),
        coeffs.reshape(modes * degrees, 2, channels),
        legendre.transpose(0, 2, 1),
        mixing,
        *constants,
    )
    result, weight = pl.pallas_call(
        kernel,
        out_shape=(
            jax.ShapeDtypeStruct((rows * lon, cols), BF16),
            jax.ShapeDtypeStruct((quads, lats, piece, channels), BF16),
        ),
        in_specs=[pl.BlockSpec(memory_space=pltpu.HBM)] * 13,
        out_specs=(pl.BlockSpec(memory_space=pltpu.HBM),) * 2,
        scratch_shapes=[
            pltpu.VMEM((rows * lon, cols), BF16),
            pltpu.VMEM((quads, lats, piece, channels), BF16),
            *[pltpu.VMEM(operand.shape, BF16) for operand in operands],
            pltpu.VMEM((channels, modes * degrees * 2), BF16),
            pltpu.VMEM((modes, held, degrees), BF16),
            pltpu.VMEM((owners, pad, LANES), BF16),
            pltpu.VMEM((chans, lats, pad, LANES), BF16),
            pltpu.VMEM((chans, lats, pad, LANES), BF16),
            pltpu.VMEM((owners, pad, LANES), BF16),
            pltpu.VMEM((quads, part, channels), BF16),
            pltpu.VMEM((quads - 1, part, channels), BF16),
            pltpu.VMEM((lats, piece, channels), F32),
            pltpu.VMEM((lats, piece, channels), BF16),
            pltpu.VMEM((lats - 1, piece, channels), BF16),
            dma((len(operands),)),
            dma((1 + quads,)),
            dma((2, 1)),
            dma((2, owners - 1)),
            dma((2, owners - 1)),
            dma((2, quads - 1)),
            dma((2, lats - 1)),
            dma((2, lats - 1)),
            dma((2, quads - 1, lats)),
        ],
        compiler_params=pltpu.CompilerParams(
            collective_id=0, has_side_effects=True, vmem_limit_bytes=60 << 20
        ),
    )(*operands)
    weight = weight.astype(F32).reshape(channels, channels) * (1.0 / (members * lon // 2))
    return result.reshape(grad_out.shape), weight


def fits(mesh, rows, lon, channels):
    lats, chans, members = (mesh.shape[axis] for axis in ("lat", "chan", "ens"))
    return (
        members == 2 and lats * chans <= 8 and rows * lon <= 512
        and lon % 16 == 0 and rows % 2 == 0
        and channels // mesh.shape["chan"] == LANES + LANES // 2
        and channels % (members * chans * lats * 8) == 0
    )


def solution(mesh):
    placed = (
        P(("grp", "ens"), "lat", None, "chan"),
        P(("grp", "ens"), "lat", None, "chan"),
        P(("grp", "ens"), ("lat", "chan"), None, None, None),
        P(("lat", "chan"), None, "ens"),
        P(),
    )

    def local(grad_out, *rest):
        rows, lon, cols = grad_out.shape[1:]
        small = fits(mesh, rows, lon, cols * mesh.shape["chan"])
        return (fused if small else on_device)(grad_out, *rest)

    return jax.shard_map(
        local,
        mesh=mesh,
        in_specs=placed,
        out_specs=(P(("grp", "ens"), "lat", None, "chan"), P("grp", None)),
        check_vma=False,
    )
```

```python
import math

import jax
import jax.numpy as jnp
import numpy as np
from jax import lax
from jax.experimental import pallas as pl
from jax.experimental.pallas import tpu as pltpu
from jax.sharding import PartitionSpec as P


def fourier_table(lon_count, mode_count):
    longitude = jnp.arange(lon_count, dtype=jnp.int32)[:, None]
    wavenumber = jnp.arange(mode_count, dtype=jnp.int32)[None, :]
    product_index = longitude * wavenumber % lon_count
    angles = 2.0 * math.pi / lon_count * product_index.astype(jnp.float32)
    factor = math.sqrt(2.0 / lon_count)
    stacked = jnp.stack([jnp.cos(angles), -jnp.sin(angles)], axis=2) * factor
    return stacked.reshape(lon_count, 2 * mode_count).astype(jnp.bfloat16)


def silu_backward(cotangent, preact):
    values = preact.astype(jnp.float32)
    gate_value = jax.nn.sigmoid(values)
    return (
        cotangent.astype(jnp.float32) * gate_value * (1.0 + values * (1.0 - gate_value))
    ).astype(jnp.bfloat16)


def on_device(grad_out, pre_act, coeffs, legendre, mixing):
    lat_rows = grad_out.shape[1]
    lon_count = grad_out.shape[2]
    chan_cols = grad_out.shape[3]
    mode_count = lon_count // 2
    lat_devices = lax.axis_size("lat")
    chan_count = lax.axis_size("chan")
    members = lax.axis_size("ens")
    lat_count = lat_rows * lat_devices
    channels = chan_cols * chan_count
    mode_width = 2 * mode_count // (lat_devices * chan_count)
    local_modes = mode_width // 2
    fourier = fourier_table(lon_count, mode_count)
    scaled = silu_backward(grad_out[0], pre_act[0])
    spectral = jnp.einsum(
        "nk,anc->akc", fourier, scaled, preferred_element_type=jnp.float32
    ).astype(jnp.bfloat16)
    exchanged = lax.all_to_all(
        lax.all_to_all(spectral, "lat", split_axis=1, concat_axis=0, tiled=True),
        "chan",
        split_axis=1,
        concat_axis=2,
        tiled=True,
    )
    spectral_modes = exchanged.reshape(lat_count, local_modes, 2, channels)
    legendre_full = lax.all_gather(legendre, "ens", axis=2, tiled=True)
    coef_grad = jnp.einsum(
        "mla,amrc->mlrc", legendre_full, spectral_modes, preferred_element_type=jnp.float32
    ).astype(jnp.bfloat16)
    stored = coeffs[0].reshape(-1, channels)
    flat_grad = coef_grad.reshape(-1, channels)
    weight_grad = lax.dot_general(
        stored, flat_grad, (((0,), (0,)), ((), ())), preferred_element_type=jnp.float32
    )
    weight_grad = weight_grad * (1.0 / (members * mode_count))
    weight_grad = lax.psum(weight_grad, ("lat", "chan", "ens"))
    mixed_grad = lax.dot_general(
        coef_grad, mixing, (((3,), (1,)), ((), ())), preferred_element_type=jnp.float32
    ).astype(jnp.bfloat16)
    returned = jnp.einsum(
        "mla,mlrc->amrc", legendre_full, mixed_grad, preferred_element_type=jnp.float32
    ).astype(jnp.bfloat16)
    shaped = returned.reshape(lat_count, 1, mode_width, channels)
    received = lax.all_to_all(
        lax.all_to_all(shaped, "lat", split_axis=0, concat_axis=1, tiled=True),
        "chan",
        split_axis=3,
        concat_axis=2,
        tiled=True,
    )
    row_coeffs = received.reshape(lat_rows, 2 * mode_count, chan_cols)
    spatial = jnp.einsum("nk,akc->anc", fourier, row_coeffs, preferred_element_type=jnp.float32)
    result = (grad_out[0].astype(jnp.float32) + spatial).astype(jnp.bfloat16)
    return (result[None], weight_grad)

MESH = pl.DeviceIdType.MESH
BF16 = jnp.bfloat16
F32 = jnp.float32


def dot(a, b, dims=((1,), (0,))):
    return lax.dot_general(a, b, (dims, ((), ())), preferred_element_type=F32)


LANES = 128


def slots(rows, width):
    whole = [(a, a, k) for a in range(rows) for k in range(width)]
    paired = [(a, a + 1, k) for a in range(0, rows, 2) for k in range(width)]
    return whole, paired


def padded(rows, width):
    return -(-(rows + rows // 2) * width // 16) * 16


def tables(rows, lon, lats, chans, members, modes, degrees):
    owners = lats * chans
    width = 2 * modes
    pad = padded(rows, width)
    n = np.arange(lon)[:, None]
    m = np.arange(lon // 2)[None, :]
    angles = np.float32(2.0 * math.pi / lon) * (n * m % lon).astype(np.float32)
    table = np.stack([np.cos(angles), -np.sin(angles)], axis=2).reshape(lon, lon)
    table = (table * np.float32(math.sqrt(2.0 / lon))).astype(np.float32)
    groups = rows + rows // 2
    inverse = np.zeros((groups, lon, owners, pad), np.float32)
    for g in range(groups):
        for d in range(owners):
            inverse[g, :, d, g * width:(g + 1) * width] = table[:, d * width:(d + 1) * width]
    inverse = inverse.reshape(groups * lon, owners * pad)
    whole, paired = slots(rows, width)
    lat_of = np.full((3, lats, pad), -1)
    key_of = np.full((3, lats, pad), -1)
    for z in range(lats):
        for i, (even, odd, k) in enumerate(whole + paired):
            if i < len(whole):
                lat_of[0, z, i], key_of[0, z, i] = z * rows + even, k
            else:
                lat_of[1, z, i], key_of[1, z, i] = z * rows + even, k
                lat_of[2, z, i], key_of[2, z, i] = z * rows + odd, k
    lat_of, key_of = lat_of.reshape(-1), key_of.reshape(-1)
    held = rows * lats // members
    select = (lat_of[None, :] == np.arange(members * held)[:, None]).astype(np.float32)
    select = select.reshape(members, held, -1)
    row = np.arange(modes * degrees * 2)
    spread = (row[:, None] // 2 == np.arange(modes * degrees)[None, :]).astype(np.float32)
    row_key = row // (2 * degrees) * 2 + row % 2
    mask = (row_key[:, None] == key_of[None, :]).astype(np.float32)
    cast = lambda x: jnp.asarray(np.ascontiguousarray(x), BF16)
    return (
        cast(inverse.T), cast(inverse), cast(select), cast(select.transpose(0, 2, 1)),
        cast(spread), cast(spread.T), cast(mask), cast(mask.T),
    )


def fused_kernel(
    lats, chans, members, lon,
    grad_hbm, pre_hbm, coeffs_hbm, leg_hbm, mix_hbm,
    fwd_hbm, inv_hbm, sel_hbm, selt_hbm, spread_hbm, spreadt_hbm, mask_hbm, maskt_hbm,
    out_hbm, full_hbm,
    out_ref, full_ref,
    grad_ref, pre_ref, coeffs_ref, leg_ref, mix_ref,
    fwd_ref, inv_ref, sel_ref, selt_ref, spread_ref, spreadt_ref, mask_ref, maskt_ref,
    stored, lbuf, sbuf, rbuf, sbuf2, rbuf2, w1s, w1r, w2own, w2s, w2r,
    isem, osem, lsem, esem, fsem, r1sem, r2sem, gsem,
):
    z, c, x = lax.axis_index("lat"), lax.axis_index("chan"), lax.axis_index("ens")
    owners, quads = lats * chans, members * chans
    me, quad = z * chans + c, x * chans + c
    pad, cols, blocks = rbuf.shape[2], grad_ref.shape[1], lats * rbuf.shape[2]

    def owner_peer(p):
        q = lax.rem(me + p, owners)
        return q, q // chans, lax.rem(q, chans)

    def quad_peer(p):
        q = lax.rem(quad + p, quads)
        return q, q // chans, lax.rem(q, chans)

    sources = (
        pre_hbm, grad_hbm, fwd_hbm, leg_hbm, sel_hbm, selt_hbm, spread_hbm, spreadt_hbm,
        mask_hbm, maskt_hbm, coeffs_hbm, mix_hbm, inv_hbm,
    )
    targets = (
        pre_ref, grad_ref, fwd_ref, leg_ref, sel_ref, selt_ref, spread_ref, spreadt_ref,
        mask_ref, maskt_ref, coeffs_ref, mix_ref, inv_ref,
    )
    loads = [
        pltpu.make_async_copy(source, target, isem.at[i])
        for i, (source, target) in enumerate(zip(sources, targets))
    ]
    for load in loads:
        load.start()
    barrier = pltpu.get_barrier_semaphore()
    for p in range(quads):
        for r in range(lats):
            if p + r > 0:
                _, px, pc = quad_peer(p)
                target = {"ens": px, "chan": pc, "lat": lax.rem(z + r, lats)}
                pl.semaphore_signal(barrier, inc=1, device_id=target, device_id_type=MESH)
    for load in loads[:4]:
        load.wait()
    values = pre_ref[...].astype(F32)
    gate = jax.nn.sigmoid(values)
    scaled = grad_ref[...].astype(F32) * gate * (1.0 + values * (1.0 - gate))
    points, half = scaled.shape[0], LANES // 2
    tail = scaled[:, LANES:].reshape(-1, 2, lon, half)
    paired = jnp.concatenate([tail[:, 0], tail[:, 1]], axis=-1).reshape(-1, LANES)
    packed = jnp.concatenate([scaled[:, :LANES], paired], axis=0).astype(BF16)
    sbuf[...] = dot(fwd_ref[...], packed).astype(BF16).reshape(owners, pad, LANES)

    pl.semaphore_wait(barrier, quads * lats - 1)

    def remote(src, dst, sems, target):
        return pltpu.make_async_remote_copy(
            src_ref=src, dst_ref=dst, send_sem=sems[0], recv_sem=sems[1],
            device_id=target, device_id_type=MESH,
        )

    def pair(sem, *index):
        return sem.at[(0,) + index], sem.at[(1,) + index]

    legs = remote(leg_ref, lbuf, pair(lsem, 0), {"ens": lax.rem(x + 1, members)})
    legs.start()
    started = [legs]
    first = []
    for p in sorted(range(1, owners), key=lambda p: abs(p - owners // 2)):
        q, pz, pc = owner_peer(p)
        copy = remote(sbuf.at[q], rbuf.at[c, z], pair(esem, p - 1), {"lat": pz, "chan": pc})
        copy.start()
        first.append(copy)
    started += first
    for load in loads[4:]:
        load.wait()
    rbuf[c, z] = sbuf[me]
    legs.wait_recv()
    other = lax.rem(x + 1, members)
    modes, degrees = leg_ref.shape[0], leg_ref.shape[2]
    by_lat, synthesis = [], 0.0
    for m in range(modes):
        mine, theirs = leg_ref[m], lbuf[m]
        down = ((0,), (0,))
        by_lat.append(dot(mine, sel_ref[x], down) + dot(theirs, sel_ref[other], down))
        by_row = dot(selt_ref[x], mine) + dot(selt_ref[other], theirs)
        rows = spreadt_ref[m * degrees:(m + 1) * degrees, :]
        synthesis = synthesis + dot(by_row.astype(BF16), rows)
    by_lat = jnp.concatenate(by_lat, axis=0).astype(BF16)
    analysis = (dot(spread_ref[...], by_lat) * mask_ref[...].astype(F32)).astype(BF16)
    synthesis = (synthesis * maskt_ref[...].astype(F32)).astype(BF16)
    across = ((1,), (1,))
    flat = coeffs_ref[...].reshape(stored.shape[::-1])
    stored[...] = flat.astype(F32).T.astype(BF16)

    for copy in first:
        copy.wait_recv()
    halves = []
    for h in range(chans):
        held = rbuf[h].reshape(blocks, LANES)
        wide, even, odd = (dot(analysis[:, v * blocks:(v + 1) * blocks], held) for v in range(3))
        halves += [wide, even[:, :half] + odd[:, half:]]
    coef = jnp.concatenate(halves, axis=1).astype(BF16)

    part = w1s.shape[1]

    def weight(q):
        return dot(stored[pl.ds(pl.multiple_of(q * part, part), part), :], coef)

    reduce1 = []
    for p in range(quads - 1, 0, -1):
        q, px, pc = quad_peer(p)
        w1s[q] = weight(q).astype(BF16)
        copy = remote(w1s.at[q], w1r.at[p - 1], pair(r1sem, p - 1), {"ens": px, "chan": pc})
        copy.start()
        reduce1.append(copy)
    started += reduce1
    own = weight(quad)

    for h in range(chans):
        mixed = dot(coef, mix_ref[h * cols:(h + 1) * cols, :], across)
        rest = mixed[:, LANES:]
        none = jnp.zeros_like(rest)
        sides = (
            mixed[:, :LANES],
            jnp.concatenate([rest, none], axis=1),
            jnp.concatenate([none, rest], axis=1),
        )
        returned = sum(
            dot(synthesis[v * blocks:(v + 1) * blocks], side.astype(BF16))
            for v, side in enumerate(sides)
        )
        sbuf2[h] = returned.astype(BF16).reshape(lats, pad, LANES)
    second = []
    for p in sorted(range(1, owners), key=lambda p: abs(p - owners // 2)):
        q, pz, pc = owner_peer(p)
        copy = remote(sbuf2.at[pc, pz], rbuf2.at[me], pair(fsem, p - 1), {"lat": pz, "chan": pc})
        copy.start()
        second.append(copy)
    started += second
    rbuf2[me] = sbuf2[c, z]

    total = own
    for p, copy in zip(range(quads - 1, 0, -1), reduce1):
        copy.wait_recv()
        total = total + w1r[p - 1].astype(F32)
    total = total.reshape(w2own.shape)
    w2own[...] = total
    w2s[...] = total.astype(BF16)
    reduce2 = []
    for p in range(1, lats):
        pz = lax.rem(z + p, lats)
        copy = remote(w2s.at[pz], w2r.at[p - 1], pair(r2sem, p - 1), {"lat": pz})
        copy.start()
        reduce2.append(copy)
    started += reduce2

    def finish():
        for copy in second:
            copy.wait_recv()
        spatial = dot(inv_ref[...], rbuf2[...].reshape(owners * pad, LANES))
        pairs = spatial[points:].reshape(-1, 1, lon, LANES)
        rest = jnp.concatenate([pairs[..., :half], pairs[..., half:]], axis=1).reshape(points, half)
        spatial = jnp.concatenate([spatial[:points], rest], axis=1)
        out_ref[...] = (grad_ref[...].astype(F32) + spatial).astype(BF16)
        stores = [pltpu.make_async_copy(out_ref, out_hbm, osem.at[0])]
        stores[0].start()
        return stores

    piece = w2own[z]
    for p, copy in enumerate(reduce2):
        copy.wait_recv()
        piece = piece + w2r[p].astype(F32)
    full_ref[quad, z] = piece.astype(BF16)
    everyone = [(p, r) for p in range(quads) for r in range(lats) if p + r > 0]
    gather = []
    for i, (p, r) in enumerate(everyone):
        _, px, pc = quad_peer(p)
        block = full_ref.at[quad, z]
        target = {"ens": px, "chan": pc, "lat": lax.rem(z + r, lats)}
        copy = remote(block, block, pair(gsem, i), target)
        copy.start()
        gather.append(copy)
    started += gather
    stores = finish()
    for copy in gather:
        copy.wait_recv()
    stores.append(pltpu.make_async_copy(full_ref, full_hbm, osem.at[1]))
    stores[1].start()
    for copy in started:
        copy.wait_send()
    for store in stores:
        store.wait()


def fused(grad_out, pre_act, coeffs, legendre, mixing):
    rows, lon, cols = grad_out.shape[1:]
    lats, chans = lax.axis_size("lat"), lax.axis_size("chan")
    members = lax.axis_size("ens")
    modes, degrees, held = legendre.shape
    owners, quads, channels = lats * chans, members * chans, cols * chans
    pad = padded(rows, 2 * modes)
    part, piece = channels // quads, channels // quads // lats
    constants = tables(rows, lon, lats, chans, members, modes, degrees)
    dma = pltpu.SemaphoreType.DMA

    def kernel(*refs):
        fused_kernel(lats, chans, members, lon, *refs)

    operands = (
        grad_out.reshape(rows * lon, cols),
        pre_act.reshape(rows * lon, cols),
        coeffs.reshape(modes * degrees, 2, channels),
        legendre.transpose(0, 2, 1),
        mixing,
        *constants,
    )
    result, weight = pl.pallas_call(
        kernel,
        out_shape=(
            jax.ShapeDtypeStruct((rows * lon, cols), BF16),
            jax.ShapeDtypeStruct((quads, lats, piece, channels), BF16),
        ),
        in_specs=[pl.BlockSpec(memory_space=pltpu.HBM)] * 13,
        out_specs=(pl.BlockSpec(memory_space=pltpu.HBM),) * 2,
        scratch_shapes=[
            pltpu.VMEM((rows * lon, cols), BF16),
            pltpu.VMEM((quads, lats, piece, channels), BF16),
            *[pltpu.VMEM(operand.shape, BF16) for operand in operands],
            pltpu.VMEM((channels, modes * degrees * 2), BF16),
            pltpu.VMEM((modes, held, degrees), BF16),
            pltpu.VMEM((owners, pad, LANES), BF16),
            pltpu.VMEM((chans, lats, pad, LANES), BF16),
            pltpu.VMEM((chans, lats, pad, LANES), BF16),
            pltpu.VMEM((owners, pad, LANES), BF16),
            pltpu.VMEM((quads, part, channels), BF16),
            pltpu.VMEM((quads - 1, part, channels), BF16),
            pltpu.VMEM((lats, piece, channels), F32),
            pltpu.VMEM((lats, piece, channels), BF16),
            pltpu.VMEM((lats - 1, piece, channels), BF16),
            dma((len(operands),)),
            dma((1 + quads,)),
            dma((2, 1)),
            dma((2, owners - 1)),
            dma((2, owners - 1)),
            dma((2, quads - 1)),
            dma((2, lats - 1)),
            dma((2, quads * lats - 1)),
        ],
        compiler_params=pltpu.CompilerParams(
            collective_id=0, has_side_effects=True, vmem_limit_bytes=60 << 20
        ),
    )(*operands)
    weight = weight.astype(F32).reshape(channels, channels) * (1.0 / (members * lon // 2))
    return result.reshape(grad_out.shape), weight


def fits(mesh, rows, lon, channels):
    lats, chans, members = (mesh.shape[axis] for axis in ("lat", "chan", "ens"))
    return (
        members == 2 and lats * chans <= 8 and rows * lon <= 512
        and lon % 16 == 0 and rows % 2 == 0
        and channels // mesh.shape["chan"] == LANES + LANES // 2
        and channels % (members * chans * lats * 8) == 0
    )


def solution(mesh):
    placed = (
        P(("grp", "ens"), "lat", None, "chan"),
        P(("grp", "ens"), "lat", None, "chan"),
        P(("grp", "ens"), ("lat", "chan"), None, None, None),
        P(("lat", "chan"), None, "ens"),
        P(),
    )

    def local(grad_out, *rest):
        rows, lon, cols = grad_out.shape[1:]
        small = fits(mesh, rows, lon, cols * mesh.shape["chan"])
        return (fused if small else on_device)(grad_out, *rest)

    return jax.shard_map(
        local,
        mesh=mesh,
        in_specs=placed,
        out_specs=(P(("grp", "ens"), "lat", None, "chan"), P("grp", None)),
        check_vma=False,
    )
```
